32 devices in a mesh: dp: 8 (over z, core), member: 4 (over y, x).
Axes of the slice: x: 2, y: 2, z: 4, core: 2. Of those that a mesh axis runs over, the one named last changes fastest.
Arguments:
- tokens: bfloat16 [1024, 4096], P('dp', 'member'), may hold values from -6 to 6
- routes: int32 [1024, 2], P('dp'), may hold values from 0 to 7, all different within a row; in each aligned block of 128 rows (0 to 127, 128 to 255, ...) at most 34 rows name the same one
- route_weights: float32 [1024, 2], P('dp'), may hold values from 0.2 to 1
- up_stacked: bfloat16 [8, 4096, 7168], P(None, ('member', 'dp')), may hold values from -0.09375 to 0.09375
- down_stacked: bfloat16 [8, 4096, 7168], P(None, ('member', 'dp')), may hold values from -0.0625 to 0.0625
- cotangent: bfloat16 [1024, 4096], P('dp', 'member'), may hold values from -6 to 6
Outputs:
- mixed: bfloat16 [1024, 4096], P('dp', 'member')
- grad_tokens: bfloat16 [1024, 4096], P('dp', 'member')
- grad_up: bfloat16 [8, 4096, 7168], P('dp', 'member')
- grad_down: bfloat16 [8, 4096, 7168], P('dp', 'member')
The draws below stay inside these ranges and needn't reach their ends.
Inputs may be any that keep to these rules, and one draw needn't show every extreme that they name: `routes`: each row names two different experts. In each aligned block of 128 rows no expert is named by more than 34 rows, and in some block some expert is named by exactly 34 rows.
All inputs are finite; a program needn't handle non-finite values.
Results may differ from the reference program's by a relative error of at most 0.018.
Values may be sent and summed in bfloat16 or wider, within the bound.
No kernel may reach another device: no remote copies, remote signals or barrier semaphores. Data moves between devices by JAX's collectives and lax.ppermute only.
A program may use at most 192 MiB of HBM per device.

```python
import math
import jax
import jax.numpy as jnp
import numpy as np
from jax import lax

D = 4096
FF_W = 7168
E = 8
TOK_DEV = 128
CAP = 34
TOKENS = 1024
N_DP = 8
N_MEMBER = 4


def block_levels(rng, extent, cuts, low, largest):
    def one(position, parts):
        draws = jax.random.uniform(jax.random.fold_in(jax.random.fold_in(rng, 6), position), (parts,), jnp.float32, low / len(cuts), largest / len(cuts))
        return jnp.repeat(jnp.exp(draws), extent[position] // parts).reshape((-1,) + (1,) * (len(extent) - position - 1))

    factor_of = one(*cuts[0])
    for cut in cuts[1:]:
        factor_of = factor_of * one(*cut)
    return factor_of


def deal_out(stream_key, own, number, rows, count, top, limit, slope):
    sequence = jax.random.permutation(stream_key, count)
    heavy_load, common = portions_of(count, rows * top, limit, slope, True), portions_of(count, rows * top, limit, slope, False)
    places = jnp.arange(count)

    def named(sizes, rotation):
        used = int((sizes > 0).sum())
        fixed = max(1, used // 4)
        moved = fixed + (places - fixed + rotation * (used - fixed)) % max(1, count - fixed)
        return jnp.zeros((count,), jnp.int32).at[sequence[jnp.where(places < fixed, places, moved)]].set(jnp.asarray(sizes, jnp.int32))

    sizes = jnp.where(number % 4 == 0, named(heavy_load, number // 4), named(common, number - number // 4 - 1))
    mixed = jax.random.permutation(jax.random.fold_in(own, 3), count)
    donor, taker = mixed[0:count // 2 * 2:2], mixed[1:count // 2 * 2:2]
    room = jnp.minimum(sizes[donor] - 1, limit - sizes[taker]) // 2
    room = jnp.where((donor == sequence[0]) | (taker == sequence[0]) | (sizes[taker] == 0), 0, jnp.maximum(room, 0))
    moved = jax.random.randint(jax.random.fold_in(own, 4), (count // 2,), 0, 1 << 20) % (room + 1)
    sizes = sizes.at[donor].add(-moved).at[taker].add(moved)
    labels = jnp.searchsorted(jnp.cumsum(sizes), jnp.arange(rows * top), side="right").astype(jnp.int32)
    listing = labels.reshape(top, rows).T
    listing = listing[jax.random.permutation(jax.random.fold_in(own, 1), rows)]
    rotation = jax.random.randint(jax.random.fold_in(own, 2), (rows, 1), 0, top)
    return jnp.take_along_axis(listing, (jnp.arange(top)[None, :] + rotation) % top, axis=1)


def portions_of(count, total, bound, skew, full):
    weights = [(1 << 20) // math.isqrt(grade ** skew) + 1 for grade in range(1, count + 1)]
    largest = bound if full else min(bound, max(-(-total // count), total * weights[0] // sum(weights)))
    least = 1 if total - largest >= count - 1 else 0
    holding, spare = [largest] + [least] * (count - 1), total - largest - least * (count - 1)
    while spare > 0:
        candidates = [i for i in range(1, count) if holding[i] < largest] or [i for i in range(1, count) if holding[i] < bound]
        pool, left = sum([weights[i] for i in candidates]), spare
        for i in candidates:
            more = min(bound - holding[i], max(1, left * weights[i] // pool), spare)
            holding[i] = holding[i] + more
            spare = spare - more
    return np.array(holding)


def scatter_about(key, shape, deviation, reach, split=(), kind=jnp.bfloat16):
    level = block_levels(key, shape, split, -0.22, 0.18) if split else 1.0
    entries = jax.random.normal(key, shape, jnp.float32) * deviation * level
    return jnp.minimum(jnp.maximum(entries, -reach), reach).astype(kind)


def setup_inputs(seed: int = 0) -> dict:
    seeds = jax.random.split(jax.random.key(seed), 7)
    tokens = scatter_about(seeds[0], (TOKENS, D), 1.0, 6.0, ((0, 8), (1, 4)))
    routes_keys = jax.random.split(jax.random.fold_in(seeds[1], 1), TOKENS // TOK_DEV)
    routes_turns = jax.random.permutation(jax.random.fold_in(seeds[1], 3), TOKENS // TOK_DEV)
    routes = jax.vmap(lambda own, number: deal_out(jax.random.fold_in(seeds[1], 2), own, number, TOK_DEV, E, 2, CAP, 2))(routes_keys, routes_turns).reshape((TOKENS, 2))
    route_weights = jnp.clip(0.2 + 0.8 * jax.random.uniform(seeds[2], (TOKENS, 2), jnp.float32) ** block_levels(seeds[2], (TOKENS, 2), ((0, 8),), -0.2, 0.2), 0.2, 1.0)
    up_stacked = scatter_about(seeds[3], (E, D, FF_W), D ** -0.5, 0.09375, ((1, 32),))
    down_stacked = scatter_about(seeds[4], (E, D, FF_W), FF_W ** -0.5, 0.0625, ((1, 32),))
    cotangent = scatter_about(seeds[5], (TOKENS, D), 1.0, 6.0, ((0, 8), (1, 4)))
    return dict(tokens=tokens, routes=routes, route_weights=route_weights, up_stacked=up_stacked, down_stacked=down_stacked, cotangent=cotangent)


def group_sum(left, right):
    row_total = left.shape[0]
    left_groups = left.astype(jnp.float32).reshape(row_total, N_MEMBER, -1)
    right_groups = right.astype(jnp.float32).reshape(N_MEMBER, -1, right.shape[1])
    partial_value = jnp.einsum("rgd,gdf->grf", left_groups, right_groups)
    rounded = lax.optimization_barrier(partial_value.astype(jnp.bfloat16))
    return jnp.sum(rounded.astype(jnp.float32), axis=0)


def owner_layout(full, quarters, hidden_own):
    return full.reshape(E, D, quarters, hidden_own).transpose(0, 2, 1, 3).reshape(E * quarters, D, hidden_own)


def reference(tokens, routes, route_weights, up_stacked, down_stacked, cotangent):
    quarters = N_DP // E
    hidden_own = FF_W // quarters
    token_total = tokens.shape[0]
    chosen = (routes[:, :, None] == jnp.arange(E, dtype=jnp.int32)[None, None, :]).astype(jnp.int32)
    blocked = chosen.reshape(N_DP, TOK_DEV * 2, E)
    before = jnp.cumsum(blocked, axis=1) - blocked
    slot_pos = jnp.sum(before * blocked, axis=2).reshape(token_total, 2).astype(jnp.int32)
    source = (jnp.arange(token_total, dtype=jnp.int32) // TOK_DEV).astype(jnp.int32)
    row_index = (source[:, None] * CAP + slot_pos).astype(jnp.int32)
    flat_index = (routes * (N_DP * CAP) + row_index).astype(jnp.int32)
    owner = jnp.full((E * N_DP * CAP,), -1, jnp.int32)
    owner = owner.at[flat_index.reshape(-1)].set(jnp.arange(token_total * 2, dtype=jnp.int32))
    owner = owner.reshape(E, N_DP * CAP)
    filled = owner >= 0
    safe_owner = jnp.maximum(owner, 0)
    token_of = safe_owner // 2
    weight_of = jnp.where(filled, route_weights.reshape(-1)[safe_owner], jnp.zeros((), jnp.float32))
    x_slots = jnp.where(filled[:, :, None], tokens[token_of], jnp.zeros((), tokens.dtype))
    d_slots = (weight_of[:, :, None] * cotangent[token_of].astype(jnp.float32)).astype(jnp.bfloat16)

    def expert(inputs):
        x_rows, d_rows, up_w, down_w = inputs
        pre = group_sum(x_rows, up_w)
        act = jax.nn.silu(pre).astype(jnp.bfloat16)
        y_rows = jnp.dot(act, down_w.T, preferred_element_type=jnp.float32)
        d_act = group_sum(d_rows, down_w)
        sig = jax.nn.sigmoid(pre)
        d_pre = (d_act * sig * (1.0 + pre * (1.0 - sig))).astype(jnp.bfloat16)
        g_down = jnp.dot(d_rows.T, act, preferred_element_type=jnp.float32).astype(jnp.bfloat16)
        g_up = jnp.dot(x_rows.T, d_pre, preferred_element_type=jnp.float32).astype(jnp.bfloat16)
        dx_rows = jnp.dot(d_pre, up_w.T, preferred_element_type=jnp.float32)
        return y_rows, dx_rows, g_up, g_down

    y_all, dx_all, g_up, g_down = lax.map(expert, (x_slots, d_slots, up_stacked, down_stacked))
    y_pick = y_all[routes, row_index]
    mixed = (route_weights[:, 0, None] * y_pick[:, 0] + route_weights[:, 1, None] * y_pick[:, 1]).astype(jnp.bfloat16)
    dx_pick = dx_all[routes, row_index]
    grad_tokens = (dx_pick[:, 0] + dx_pick[:, 1]).astype(jnp.bfloat16)
    return mixed, grad_tokens, owner_layout(g_up, quarters, hidden_own), owner_layout(g_down, quarters, hidden_own)
```

```python
import functools

import jax
import jax.numpy as jnp
from jax import lax
from jax.experimental import pallas as pl
from jax.experimental.pallas import tpu as pltpu
from jax.sharding import PartitionSpec as P


FF_W = 7168
E = 8
CAP = 34
HALVES = 2
LANES = 128
BF = jnp.bfloat16
F32 = jnp.float32


def contract(left, right, left_dim, right_dim):
    return lax.dot_general(
        left, right, (((left_dim,), (right_dim,)), ((), ())), preferred_element_type=jnp.float32
    )


def plain_body(tokens, routes, route_weights, up_stacked, down_stacked, cotangent):
    dp_count = lax.axis_size("dp")
    member_count = lax.axis_size("member")
    quarters = dp_count // E
    share_rows = up_stacked.shape[1]
    features = tokens.shape[1]
    hidden_own = FF_W // quarters
    per_member = hidden_own // member_count
    slots_all = E * CAP
    up_parts = (
        up_stacked.reshape(E, share_rows, quarters, hidden_own)
        .transpose(0, 2, 1, 3)
        .reshape(dp_count, share_rows, hidden_own)
    )
    down_parts = (
        down_stacked.reshape(E, share_rows, quarters, hidden_own)
        .transpose(0, 2, 1, 3)
        .reshape(dp_count, share_rows, hidden_own)
    )
    up_own, down_own = (
        lax.all_to_all(up_parts, "dp", split_axis=0, concat_axis=1, tiled=True),
        lax.all_to_all(down_parts, "dp", split_axis=0, concat_axis=1, tiled=True),
    )
    up_own = up_own.reshape(dp_count * share_rows, hidden_own)
    down_own = down_own.reshape(dp_count * share_rows, hidden_own)
    chosen = (routes[:, :, None] == jnp.arange(E, dtype=jnp.int32)[None, None, :]).astype(jnp.int32)
    flat_hits = chosen.reshape(-1, E)
    before = jnp.cumsum(flat_hits, axis=0) - flat_hits
    slot_pos = jnp.sum(before * flat_hits, axis=1).reshape(-1, 2)
    target = routes * CAP + slot_pos
    slot_hits = jnp.arange(slots_all, dtype=jnp.int32)[:, None, None] == target[None, :, :]
    pick_table = jnp.sum(slot_hits.astype(jnp.float32), axis=2)
    weighted = jnp.sum(jnp.where(slot_hits, route_weights[None, :, :], 0.0), axis=2)
    x_local = jnp.dot(
        pick_table.astype(jnp.bfloat16), tokens, preferred_element_type=jnp.float32
    ).astype(jnp.bfloat16)
    d_local = jnp.dot(
        weighted, cotangent.astype(jnp.float32), precision=lax.Precision.HIGHEST
    ).astype(jnp.bfloat16)

    def spread(local):
        return jnp.broadcast_to(
            local.reshape(E, 1, CAP, features), (E, quarters, CAP, features)
        ).reshape(dp_count, CAP, features)

    def collect(returned):
        return jnp.sum(returned.reshape(E, quarters, CAP, features), axis=1).reshape(
            slots_all, features
        )

    x_in = lax.all_to_all(spread(x_local), "dp", split_axis=0, concat_axis=0, tiled=True).reshape(
        dp_count * CAP, features
    )
    partial_value = jnp.dot(x_in, up_own, preferred_element_type=jnp.float32).astype(jnp.bfloat16)
    pre_full = lax.psum(partial_value, "member").astype(jnp.float32)
    act_full = jax.nn.silu(pre_full).astype(jnp.bfloat16)
    y_part = contract(act_full, down_own, 1, 1)
    y_back = lax.all_to_all(
        y_part.reshape(dp_count, CAP, features).astype(jnp.bfloat16),
        "dp",
        split_axis=0,
        concat_axis=0,
        tiled=True,
    ).astype(jnp.float32)
    d_in = lax.all_to_all(spread(d_local), "dp", split_axis=0, concat_axis=0, tiled=True).reshape(
        dp_count * CAP, features
    )
    d_act = lax.psum_scatter(
        contract(down_own, d_in, 0, 1).astype(jnp.bfloat16),
        "member",
        scatter_dimension=0,
        tiled=True,
    ).astype(jnp.float32)
    own_start = lax.axis_index("member") * per_member
    pre_share = lax.dynamic_slice_in_dim(pre_full, own_start, per_member, 1).T
    sigma = jax.nn.sigmoid(pre_share)
    d_share = (d_act * sigma * (1.0 + pre_share * (1.0 - sigma))).astype(jnp.bfloat16)
    d_pre = lax.all_gather(d_share, "member", axis=0, tiled=True)
    g_down = contract(d_in, act_full, 0, 0)
    g_up = contract(x_in, d_pre, 0, 1)
    dx_part = contract(d_pre, up_own, 0, 1)
    dx_back = lax.all_to_all(
        dx_part.reshape(dp_count, CAP, features).astype(jnp.bfloat16),
        "dp",
        split_axis=0,
        concat_axis=0,
        tiled=True,
    ).astype(jnp.float32)
    y_slots = collect(y_back)
    dx_slots = collect(dx_back)
    mixed = jnp.dot(weighted.T, y_slots, precision=lax.Precision.HIGHEST).astype(jnp.bfloat16)
    grad_tokens = jnp.dot(pick_table.T, dx_slots, precision=lax.Precision.HIGHEST).astype(
        jnp.bfloat16
    )
    grad_up = g_up.astype(jnp.bfloat16).reshape(1, features, hidden_own)
    grad_down = g_down.astype(jnp.bfloat16).reshape(1, features, hidden_own)
    return (mixed, grad_tokens, grad_up, grad_down)


def slot_rows(routes_ref):
    tok = routes_ref.shape[1]
    expert = lax.broadcasted_iota(jnp.int32, (E, tok), 0)
    hits = [(routes_ref[k : k + 1, :] == expert) for k in range(2)]
    either = jnp.where(hits[0] | hits[1], 1.0, 0.0).astype(BF)
    earlier = lax.broadcasted_iota(jnp.int32, (tok, tok), 0) < lax.broadcasted_iota(
        jnp.int32, (tok, tok), 1
    )
    before = jnp.dot(either, jnp.where(earlier, 1.0, 0.0).astype(BF), preferred_element_type=F32)
    return [jnp.where(hit, before, -1.0) for hit in hits]


def slot_hits(rows, e):
    slot = lax.broadcasted_iota(jnp.int32, (CAP, rows[0].shape[1]), 0).astype(F32)
    return [jnp.where(slot == rows[k][e : e + 1, :], 1.0, 0.0) for k in range(2)]


def route_kernel(routes_ref, weights_ref, tokens_ref, cot_ref, out_ref):
    features = tokens_ref.shape[1]
    size = out_ref.shape[0] // HALVES
    half = features // HALVES
    rows = slot_rows(routes_ref)
    for e in range(E):
        at = slot_hits(rows, e)
        pick = (at[0] + at[1]).astype(BF)
        scale = jnp.sum(at[0] * weights_ref[0:1, :] + at[1] * weights_ref[1:2, :], 1, keepdims=True)
        x_rows = jnp.dot(pick, tokens_ref[...], preferred_element_type=F32).astype(BF)
        d_rows = (scale * jnp.dot(pick, cot_ref[...], preferred_element_type=F32)).astype(BF)
        other = e ^ size
        cut = (other // size) * half
        for i, value in enumerate((x_rows, d_rows)):
            out_ref[e, :, i * features : (i + 1) * features] = value
            out_ref[other, :, 2 * features + i * half : 2 * features + (i + 1) * half] = value[
                :, cut : cut + half
            ]


def route(routes_t, weights_t, tokens, cotangent, dp_count):
    features = tokens.shape[1]
    return pl.pallas_call(
        route_kernel,
        out_shape=jax.ShapeDtypeStruct((dp_count, CAP, 3 * features), BF),
        cost_estimate=pl.CostEstimate(
            flops=4 * E * CAP * tokens.size, bytes_accessed=2 * 10 * tokens.size, transcendentals=0
        ),
        name="route",
    )(routes_t, weights_t, tokens, cotangent)


def returned_rows(ref, e, half, kind):
    size, width = ref.shape[0] // HALVES, ref.shape[2] // 4
    if e // size == half:
        return ref[e, :, kind * width : (kind + 1) * width]
    return ref[e ^ size, :, (2 + kind) * width : (3 + kind) * width]


def mix_kernel(routes_ref, weights_ref, back_ref, mixed_ref, grad_ref):
    tok = routes_ref.shape[1]
    rows = slot_rows(routes_ref)
    width = back_ref.shape[2] // 4
    for half in range(HALVES):
        first, second, grad = [jnp.zeros((tok, width), F32) for _ in range(3)]
        for e in range(E):
            at = [hit.astype(BF) for hit in slot_hits(rows, e)]
            y_rows = returned_rows(back_ref, e, half, 0)
            first += contract(at[0], y_rows, 0, 0)
            second += contract(at[1], y_rows, 0, 0)
            grad += contract(at[0] + at[1], returned_rows(back_ref, e, half, 1), 0, 0)
        lanes = slice(half * width, (half + 1) * width)
        mixed_ref[:, lanes] = (weights_ref[:, 0:1] * first + weights_ref[:, 1:2] * second).astype(BF)
        grad_ref[:, lanes] = grad.astype(BF)


def full_spec(shape):
    return pl.BlockSpec(shape, lambda q, where: (0,) * len(shape))


class Plan:
    def __init__(self, dp_count, members, share, hidden):
        self.dp_count, self.members, self.share, self.hidden = dp_count, members, share, hidden
        self.size = dp_count // HALVES
        self.peers = self.size - 1
        self.group_features = self.size * share
        self.slots = dp_count * CAP
        self.where = jnp.stack([lax.axis_index("dp"), lax.axis_index("member")]).astype(jnp.int32)
        self.last = None

    def part(self, where, p, k=0):
        return (where[0] ^ (p * self.size)) ^ k

    def swap(self, value, k):
        return lax.ppermute(value, "dp", [(i, i ^ k) for i in range(self.dp_count)])

    def pass_on(self, value, k):
        return lax.ppermute(value, "member", [(i, i ^ k) for i in range(self.members)])

    def call(self, kernel, grid, in_specs, args, out_specs, out_shape, cost, aliases=None, scratch=()):
        args, in_specs = list(args), list(in_specs)
        if self.last is not None and not any(arg is self.last for arg in args):
            args.append(self.last)
            in_specs.append(pl.BlockSpec(memory_space=pl.ANY))

            def placed(where, *refs, count=len(args) - 1):
                kernel(where, *refs[:count], *refs[count + 1 :])
        else:
            placed = kernel
        outs = pl.pallas_call(
            placed,
            grid_spec=pltpu.PrefetchScalarGridSpec(
                num_scalar_prefetch=1,
                grid=grid,
                in_specs=in_specs,
                out_specs=out_specs,
                scratch_shapes=scratch,
            ),
            out_shape=out_shape,
            input_output_aliases={i + 1: o for i, o in (aliases or {}).items()},
            cost_estimate=pl.CostEstimate(flops=cost[0], bytes_accessed=cost[1], transcendentals=0),
        )(self.where, *args)
        self.last = outs[-1]
        return outs


def prepare(plan, got):
    features = got.shape[2] // 3
    half, share, slots = plan.group_features, plan.share, plan.slots

    def kernel(where, got_ref, own_ref, rows_ref, wide_ref):
        place, group = where[0] % plan.size, where[0] // plan.size
        for b in range(plan.dp_count):
            wide_ref[b * CAP : (b + 1) * CAP, :] = got_ref[b].astype(F32)
        for i in range(2):
            own_ref[i] = wide_ref[:, i * features : (i + 1) * features].astype(BF)
            for k in range(plan.size):
                into = slice(k * share, (k + 1) * share)
                shift = (place ^ k) * share
                for p, base in ((0, i * features + group * half), (1, 2 * features + i * half)):
                    at = pl.multiple_of(base + shift, LANES)
                    rows_ref[2 * p + i, :, into] = wide_ref[:, pl.ds(at, share)].astype(BF)

    return plan.call(
        kernel,
        (1,),
        [full_spec(got.shape)],
        [got],
        [full_spec((2, slots, features)), full_spec((4, slots, half))],
        [
            jax.ShapeDtypeStruct((2, slots, features), BF),
            jax.ShapeDtypeStruct((4, slots, half), BF),
        ],
        (0, 6 * got.size),
        scratch=[pltpu.VMEM((slots, got.shape[2]), F32)],
    )


def pack(plan, up, down, start, width):
    step = plan.members * LANES
    first = start // step

    def kernel(where, *refs):
        del where
        sources, outs = refs[: plan.peers * 4], refs[-plan.peers :]
        for k in range(plan.peers):
            for i in range(4):
                outs[k][i] = sources[k * 4 + i][0]

    in_specs = [
        pl.BlockSpec(
            (1, plan.share, step),
            functools.partial(lambda i, where, p, k: (plan.part(where, p, k), 0, first + i), p=p, k=k),
        )
        for k in range(1, plan.size)
        for p in range(HALVES)
        for _ in range(2)
    ]
    return plan.call(
        kernel,
        (width // step,),
        in_specs,
        [up, down] * (plan.peers * HALVES),
        [
            pl.BlockSpec((4, plan.share, step), lambda i, where: (0, 0, i))
            for _ in range(plan.peers)
        ],
        [jax.ShapeDtypeStruct((4, plan.share, width), BF) for _ in range(plan.peers)],
        (0, plan.peers * 4 * plan.share * width * 4),
    )


def weight_specs(plan, start, width):
    own = pl.BlockSpec(
        (1, plan.share, width), lambda p, where: (plan.part(where, p), 0, start // width)
    )
    return [own, own] + [
        pl.BlockSpec((2, plan.share, width), lambda p, where: (p, 0, 0)) for _ in range(plan.peers)
    ]


def member_lanes(where, m, sub):
    return pl.ds(pl.multiple_of((where[1] ^ m) * sub, LANES), sub)


def stacked_rows(refs, i, lanes):
    return jnp.concatenate([refs[i][0, :, lanes]] + [ref[i, :, lanes] for ref in refs[2:]], axis=0)


def hidden_partials(plan, rows, up, down, came, start, width):
    sub = width // plan.members
    half, slots = plan.group_features, plan.slots

    def kernel(where, rows_ref, *refs):
        w_refs, outs = refs[: 2 + plan.peers], refs[-plan.members :]
        for m in range(plan.members):
            lanes = member_lanes(where, m, sub)
            for i in range(2):
                outs[m][i] = jnp.dot(
                    rows_ref[i], stacked_rows(w_refs, i, lanes), preferred_element_type=F32
                ).astype(BF)

    return plan.call(
        kernel,
        (HALVES,),
        [pl.BlockSpec((2, slots, half), lambda p, where: (p, 0, 0))]
        + weight_specs(plan, start, width),
        [rows, up, down, *came],
        [pl.BlockSpec((2, slots, sub), lambda p, where: (p, 0, 0)) for _ in range(plan.members)],
        [jax.ShapeDtypeStruct((4, slots, sub), BF) for _ in range(plan.members)],
        (8 * slots * half * width, 8 * width * (slots + half)),
    )


def sum_away(plan, parts):
    _, slots, sub = parts[0].shape

    def kernel(where, *refs):
        del where
        total = refs[0][0].astype(F32)
        for ref in refs[1 : plan.members]:
            total += ref[0].astype(F32)
        refs[-1][0] = total.astype(BF)

    return plan.call(
        kernel,
        (2,),
        [pl.BlockSpec((1, slots, sub), lambda q, where: (2 + q, 0, 0))] * plan.members,
        parts,
        [pl.BlockSpec((1, slots, sub), lambda q, where: (q, 0, 0))],
        [jax.ShapeDtypeStruct((2, slots, sub), BF)],
        (0, 4 * slots * sub * (plan.members + 1)),
    )[0]


def activate(plan, parts, back):
    _, slots, sub = parts[0].shape
    lanes = min(sub, 2 * LANES)

    def kernel(where, *refs):
        del where
        sums = []
        for i in range(2):
            total = refs[plan.members][i].astype(F32)
            for ref in refs[: plan.members]:
                total += ref[i].astype(F32)
            sums.append(total)
        pre, d_act = sums
        sigma = 1.0 / (1.0 + jnp.exp(-pre))
        refs[-1][0] = (pre * sigma).astype(BF)
        refs[-1][1] = (d_act * sigma * (1.0 + pre * (1.0 - sigma))).astype(BF)

    spec = pl.BlockSpec((2, slots, lanes), lambda q, where: (0, 0, q))
    return plan.call(
        kernel,
        (sub // lanes,),
        [spec] * (plan.members + 1),
        [*parts, back],
        [spec],
        [jax.ShapeDtypeStruct((2, slots, sub), BF)],
        (0, 4 * slots * sub * (plan.members + 2)),
    )[0]


def feature_sums(plan, total, pieces, up, down, came, start, width, final):
    sub = width // plan.members
    half, share, slots = plan.group_features, plan.share, plan.slots

    def kernel(where, *refs):
        place = where[0] % plan.size
        p_refs = refs[: plan.members]
        w_refs = refs[plan.members : plan.members + 2 + plan.peers]
        before = refs[plan.members + 2 + plan.peers]
        out = refs[-2] if final else refs[-1]
        for i in range(2):
            value = None
            for m in range(plan.members):
                weights = stacked_rows(w_refs, 1 - i, member_lanes(where, m, sub))
                term = contract(p_refs[m][i], weights, 1, 1)
                value = term if value is None else value + term
            for k in range(plan.size):
                at = pl.ds(pl.multiple_of((place ^ k) * share, LANES), share)
                piece = value[:, k * share : (k + 1) * share]
                if total is not None:
                    piece += before[i, :, at]
                if final:
                    refs[-1][:, at] = piece
                else:
                    out[i, :, at] = piece
            if final:
                for b in range(plan.dp_count):
                    out[b, :, i * half : (i + 1) * half] = refs[-1][
                        b * CAP : (b + 1) * CAP, :
                    ].astype(BF)

    stack = pl.BlockSpec((2, slots, half), lambda p, where: (p, 0, 0))
    in_specs = [
        pl.BlockSpec((2, slots, sub), lambda p, where: (p, 0, 0)) for _ in range(plan.members)
    ] + weight_specs(plan, start, width)
    args = [*pieces, up, down, *came]
    if total is not None:
        in_specs.append(stack)
        args.append(total)
    if final:
        out_spec = pl.BlockSpec((plan.dp_count, CAP, 2 * half), lambda p, where: (0, 0, p))
        out = jax.ShapeDtypeStruct((plan.dp_count, CAP, 4 * half), BF)
    else:
        out_spec, out = stack, jax.ShapeDtypeStruct((4, slots, half), F32)
    return plan.call(
        kernel,
        (HALVES,),
        in_specs,
        args,
        [out_spec],
        [out],
        (8 * slots * half * width, 8 * width * (slots + half) + 32 * slots * half),
        scratch=[pltpu.VMEM((slots, half), F32)] if final else (),
    )[0]


def weight_grads(plan, buffers, x_t, d_t, pieces, start, width):
    sub = width // plan.members
    features, slots = x_t.shape
    block = features // 2

    def kernel(where, x_ref, d_ref, *refs):
        up_out, down_out = refs[-2:]
        for m in range(plan.members):
            lanes = member_lanes(where, m, sub)
            down_out[0, :, lanes] = jnp.dot(
                d_ref[...], refs[m][0], preferred_element_type=F32
            ).astype(BF)
            up_out[0, :, lanes] = jnp.dot(
                x_ref[...], refs[m][1], preferred_element_type=F32
            ).astype(BF)

    in_specs = [pl.BlockSpec((block, slots), lambda q, where: (q, 0))] * 2
    in_specs += [full_spec((2, slots, sub))] * plan.members
    args = [x_t, d_t, *pieces]
    aliases = {}
    if buffers is not None:
        aliases = {len(args): 0, len(args) + 1: 1}
        in_specs += [pl.BlockSpec(memory_space=pl.ANY)] * 2
        args += buffers
    return plan.call(
        kernel,
        (2,),
        in_specs,
        args,
        [pl.BlockSpec((1, block, width), lambda q, where: (0, q, start // width))] * 2,
        [jax.ShapeDtypeStruct((1, features, plan.hidden), BF) for _ in range(2)],
        (4 * features * slots * width, 4 * width * (slots + features)),
        aliases=aliases,
    )


def chunk_list(hidden, unit):
    units = hidden // unit
    wide = max(0, (units - 1) // 2)
    narrow = [(2 * wide + i, 1) for i in range(units - 2 * wide)]
    chunks = narrow[:-1] + [(2 * i, 2) for i in range(wide)] + narrow[-1:]
    return [(unit * start, unit * width) for start, width in chunks]


LAGS = (
    ("hidden", 0),
    ("spread", 2),
    ("activate", 1),
    ("features", 3),
    ("away", 0),
    ("fetch", -2),
    ("grads", 5),
)


def order_of(count):
    steps = [("fetch", 0), ("route", 0), ("fetch", 1), ("prepare", 0)]
    for i in range(count + max(lag for _, lag in LAGS)):
        for kind, lag in LAGS:
            first = 2 if kind == "fetch" else 0
            if first <= i - lag < count:
                steps.append((kind, i - lag))
                if (kind, i - lag) == ("features", count - 1):
                    steps.append(("return", 0))
    return steps


def halves_body(tokens, routes, route_weights, up, down, cotangent):
    dp_count, members = lax.axis_size("dp"), lax.axis_size("member")
    share, hidden = up.shape[1:]
    plan = Plan(dp_count, members, share, hidden)

    chunks = chunk_list(hidden, members * LANES)
    count = len(chunks)
    routes_t, weights_t = routes.T, route_weights.T

    came, reduced, backs, owns, others, pieces = {}, {}, {}, {}, {}, {}
    got = own = rows = total = grads = back = None
    for kind, i in order_of(count):
        if kind == "fetch":
            packed = pack(plan, up, down, *chunks[i])
        elif kind == "route":
            send = route(routes_t, weights_t, tokens, cotangent, dp_count)
        elif kind == "prepare":
            own, rows = prepare(plan, got)
        elif kind == "hidden":
            outs = hidden_partials(plan, rows, up, down, came[i], *chunks[i])
        elif kind == "away":
            away = sum_away(plan, reduced[i])
        elif kind == "activate":
            owns[i] = activate(plan, reduced[i], backs[i])
        elif kind == "spread":
            both = jnp.concatenate([owns[i], others[i]], axis=0)
        elif kind == "features":
            total = feature_sums(
                plan, total, pieces[i], up, down, came[i], *chunks[i], i == count - 1
            )
        elif kind == "grads":
            grads = weight_grads(plan, grads, x_t, d_t, pieces[i], *chunks[i])
        if kind == "fetch":
            came[i] = [plan.swap(packed[k], k + 1) for k in range(plan.peers)]
        elif kind == "route":
            got = lax.all_to_all(send, "dp", split_axis=0, concat_axis=0, tiled=True)
        elif kind == "prepare":
            x_t, d_t = own[0].T, own[1].T
        elif kind == "hidden":
            reduced[i] = [outs[0]] + [plan.pass_on(outs[k], k) for k in range(1, members)]
        elif kind == "away":
            backs[i] = plan.swap(away, plan.size)
        elif kind == "activate":
            others[i] = plan.swap(owns[i], plan.size)
        elif kind == "spread":
            pieces[i] = [both] + [plan.pass_on(both, k) for k in range(1, members)]
        elif kind == "return":
            back = lax.all_to_all(total, "dp", split_axis=0, concat_axis=0, tiled=True)

    out = jax.ShapeDtypeStruct(tokens.shape, BF)
    mixed, grad_tokens = pl.pallas_call(mix_kernel, out_shape=(out, out), name="mix")(
        routes_t, route_weights, back
    )
    return (mixed, grad_tokens, *grads)


def power_of_two(value):
    return value & (value - 1) == 0


def solution(mesh):
    placed = (
        P("dp", "member"),
        P("dp", None),
        P("dp", None),
        P(None, ("member", "dp"), None),
        P(None, ("member", "dp"), None),
        P("dp", "member"),
    )

    dp_count, members = mesh.shape["dp"], mesh.shape["member"]
    fits = (
        dp_count == E
        and power_of_two(members)
        and FF_W % (members * LANES) == 0
    )

    def body(*args):
        if not fits or args[3].shape[1] % LANES:
            return plain_body(*args)
        return halves_body(*args)

    return jax.shard_map(
        body,
        mesh=mesh,
        in_specs=placed,
        out_specs=(
            P("dp", "member"),
            P("dp", "member"),
            P("dp", "member", None),
            P("dp", "member", None),
        ),
        check_vma=False,
    )
```

```python
import functools

import jax
import jax.numpy as jnp
from jax import lax
from jax.experimental import pallas as pl
from jax.experimental.pallas import tpu as pltpu
from jax.sharding import PartitionSpec as P


FF_W = 7168
E = 8
CAP = 34
HALVES = 2
GRAD_STEPS = 4
LANES = 128
SUBLANES = 8
NOWHERE = -1e6
BF = jnp.bfloat16
F32 = jnp.float32


def contract(left, right, left_dim, right_dim):
    return lax.dot_general(
        left, right, (((left_dim,), (right_dim,)), ((), ())), preferred_element_type=jnp.float32
    )


def plain_body(tokens, routes, route_weights, up_stacked, down_stacked, cotangent):
    dp_count = lax.axis_size("dp")
    member_count = lax.axis_size("member")
    quarters = dp_count // E
    share_rows = up_stacked.shape[1]
    features = tokens.shape[1]
    hidden_own = FF_W // quarters
    per_member = hidden_own // member_count
    slots_all = E * CAP
    up_parts = (
        up_stacked.reshape(E, share_rows, quarters, hidden_own)
        .transpose(0, 2, 1, 3)
        .reshape(dp_count, share_rows, hidden_own)
    )
    down_parts = (
        down_stacked.reshape(E, share_rows, quarters, hidden_own)
        .transpose(0, 2, 1, 3)
        .reshape(dp_count, share_rows, hidden_own)
    )
    up_own, down_own = (
        lax.all_to_all(up_parts, "dp", split_axis=0, concat_axis=1, tiled=True),
        lax.all_to_all(down_parts, "dp", split_axis=0, concat_axis=1, tiled=True),
    )
    up_own = up_own.reshape(dp_count * share_rows, hidden_own)
    down_own = down_own.reshape(dp_count * share_rows, hidden_own)
    chosen = (routes[:, :, None] == jnp.arange(E, dtype=jnp.int32)[None, None, :]).astype(jnp.int32)
    flat_hits = chosen.reshape(-1, E)
    before = jnp.cumsum(flat_hits, axis=0) - flat_hits
    slot_pos = jnp.sum(before * flat_hits, axis=1).reshape(-1, 2)
    target = routes * CAP + slot_pos
    slot_hits = jnp.arange(slots_all, dtype=jnp.int32)[:, None, None] == target[None, :, :]
    pick_table = jnp.sum(slot_hits.astype(jnp.float32), axis=2)
    weighted = jnp.sum(jnp.where(slot_hits, route_weights[None, :, :], 0.0), axis=2)
    x_local = jnp.dot(
        pick_table.astype(jnp.bfloat16), tokens, preferred_element_type=jnp.float32
    ).astype(jnp.bfloat16)
    d_local = jnp.dot(
        weighted, cotangent.astype(jnp.float32), precision=lax.Precision.HIGHEST
    ).astype(jnp.bfloat16)

    def spread(local):
        return jnp.broadcast_to(
            local.reshape(E, 1, CAP, features), (E, quarters, CAP, features)
        ).reshape(dp_count, CAP, features)

    def collect(returned):
        return jnp.sum(returned.reshape(E, quarters, CAP, features), axis=1).reshape(
            slots_all, features
        )

    x_in = lax.all_to_all(spread(x_local), "dp", split_axis=0, concat_axis=0, tiled=True).reshape(
        dp_count * CAP, features
    )
    partial_value = jnp.dot(x_in, up_own, preferred_element_type=jnp.float32).astype(jnp.bfloat16)
    pre_full = lax.psum(partial_value, "member").astype(jnp.float32)
    act_full = jax.nn.silu(pre_full).astype(jnp.bfloat16)
    y_part = contract(act_full, down_own, 1, 1)
    y_back = lax.all_to_all(
        y_part.reshape(dp_count, CAP, features).astype(jnp.bfloat16),
        "dp",
        split_axis=0,
        concat_axis=0,
        tiled=True,
    ).astype(jnp.float32)
    d_in = lax.all_to_all(spread(d_local), "dp", split_axis=0, concat_axis=0, tiled=True).reshape(
        dp_count * CAP, features
    )
    d_act = lax.psum_scatter(
        contract(down_own, d_in, 0, 1).astype(jnp.bfloat16),
        "member",
        scatter_dimension=0,
        tiled=True,
    ).astype(jnp.float32)
    own_start = lax.axis_index("member") * per_member
    pre_share = lax.dynamic_slice_in_dim(pre_full, own_start, per_member, 1).T
    sigma = jax.nn.sigmoid(pre_share)
    d_share = (d_act * sigma * (1.0 + pre_share * (1.0 - sigma))).astype(jnp.bfloat16)
    d_pre = lax.all_gather(d_share, "member", axis=0, tiled=True)
    g_down = contract(d_in, act_full, 0, 0)
    g_up = contract(x_in, d_pre, 0, 1)
    dx_part = contract(d_pre, up_own, 0, 1)
    dx_back = lax.all_to_all(
        dx_part.reshape(dp_count, CAP, features).astype(jnp.bfloat16),
        "dp",
        split_axis=0,
        concat_axis=0,
        tiled=True,
    ).astype(jnp.float32)
    y_slots = collect(y_back)
    dx_slots = collect(dx_back)
    mixed = jnp.dot(weighted.T, y_slots, precision=lax.Precision.HIGHEST).astype(jnp.bfloat16)
    grad_tokens = jnp.dot(pick_table.T, dx_slots, precision=lax.Precision.HIGHEST).astype(
        jnp.bfloat16
    )
    grad_up = g_up.astype(jnp.bfloat16).reshape(1, features, hidden_own)
    grad_down = g_down.astype(jnp.bfloat16).reshape(1, features, hidden_own)
    return (mixed, grad_tokens, grad_up, grad_down)


def slot_rows(routes_ref):
    tok = routes_ref.shape[1]
    expert = lax.broadcasted_iota(jnp.int32, (E, tok), 0)
    hits = [(routes_ref[k : k + 1, :] == expert) for k in range(2)]
    either = jnp.where(hits[0] | hits[1], 1.0, 0.0).astype(BF)
    earlier = lax.broadcasted_iota(jnp.int32, (tok, tok), 0) < lax.broadcasted_iota(
        jnp.int32, (tok, tok), 1
    )
    before = jnp.dot(either, jnp.where(earlier, 1.0, 0.0).astype(BF), preferred_element_type=F32)
    return [jnp.where(hit, before, NOWHERE) for hit in hits]


def padded(rows):
    return -(-rows // SUBLANES) * SUBLANES


def slot_hits(rows, e, count=CAP, base=0):
    slot = lax.broadcasted_iota(jnp.int32, (count, rows[0].shape[1]), 0).astype(F32)
    return [jnp.where(slot == rows[k][e : e + 1, :] + base, 1.0, 0.0) for k in range(2)]


def route_kernel(routes_ref, weights_ref, tokens_ref, cot_ref, out_ref, wide_ref):
    features = tokens_ref.shape[1]
    size = out_ref.shape[0] // HALVES
    half = features // HALVES
    rows = slot_rows(routes_ref)
    for e in range(E):
        at = slot_hits(rows, e)
        pick = (at[0] + at[1]).astype(BF)
        scale = jnp.sum(at[0] * weights_ref[0:1, :] + at[1] * weights_ref[1:2, :], 1, keepdims=True)
        x_rows = jnp.dot(pick, tokens_ref[...], preferred_element_type=F32)
        d_rows = scale * jnp.dot(pick, cot_ref[...], preferred_element_type=F32)
        other = e ^ size
        cut = (other // size) * half
        for i, value in enumerate((x_rows, d_rows)):
            wide_ref[e, i * CAP : (i + 1) * CAP, :] = value
            wide_ref[other, 2 * CAP : 3 * CAP, i * half : (i + 1) * half] = value[:, cut : cut + half]
    extra = out_ref.shape[1] - 3 * CAP
    for e in range(E):
        if extra:
            wide_ref[e, 3 * CAP :, :] = jnp.zeros((extra, features), F32)
        out_ref[e] = wide_ref[e].astype(BF)


def route(routes_t, weights_t, tokens, cotangent, dp_count):
    features = tokens.shape[1]
    return pl.pallas_call(
        route_kernel,
        out_shape=jax.ShapeDtypeStruct((dp_count, padded(3 * CAP), features), BF),
        scratch_shapes=[pltpu.VMEM((dp_count, padded(3 * CAP), features), F32)],
        cost_estimate=pl.CostEstimate(
            flops=4 * E * CAP * tokens.size, bytes_accessed=2 * 10 * tokens.size, transcendentals=0
        ),
        name="route",
    )(routes_t, weights_t, tokens, cotangent)


def returned(size, e, half, kind):
    near = e // size == half
    return (e if near else e ^ size), (kind if near else 2 + kind) * CAP


def mix_kernel(routes_ref, weights_ref, back_ref, mixed_ref, grad_ref):
    tok = routes_ref.shape[1]
    rows = slot_rows(routes_ref)
    owners, count, width = back_ref.shape
    for half in range(HALVES):
        first, second, grad = [jnp.zeros((tok, width), F32) for _ in range(3)]
        for e in range(E):
            owner, base = returned(owners // HALVES, e, half, 0)
            at = slot_hits(rows, e, count, base)
            first += contract(at[0].astype(BF), back_ref[owner], 0, 0)
            second += contract(at[1].astype(BF), back_ref[owner], 0, 0)
            owner, base = returned(owners // HALVES, e, half, 1)
            at = slot_hits(rows, e, count, base)
            grad += contract((at[0] + at[1]).astype(BF), back_ref[owner], 0, 0)
        lanes = slice(half * width, (half + 1) * width)
        mixed_ref[:, lanes] = (weights_ref[:, 0:1] * first + weights_ref[:, 1:2] * second).astype(BF)
        grad_ref[:, lanes] = grad.astype(BF)


def full_spec(shape):
    return pl.BlockSpec(shape, lambda q, where: (0,) * len(shape))


class Plan:
    def __init__(self, dp_count, members, share, hidden):
        self.dp_count, self.members, self.share, self.hidden = dp_count, members, share, hidden
        self.size = dp_count // HALVES
        self.peers = self.size - 1
        self.group_features = self.size * share
        self.slots = dp_count * CAP
        self.where = jnp.stack([lax.axis_index("dp"), lax.axis_index("member")]).astype(jnp.int32)
        self.last = None

    def part(self, where, p, k=0):
        return (where[0] ^ (p * self.size)) ^ k

    def swap(self, value, k):
        return lax.ppermute(value, "dp", [(i, i ^ k) for i in range(self.dp_count)])

    def pass_on(self, value, k):
        return lax.ppermute(value, "member", [(i, i ^ k) for i in range(self.members)])

    def call(self, kernel, grid, in_specs, args, out_specs, out_shape, cost, aliases=None, scratch=()):
        args, in_specs = list(args), list(in_specs)
        if self.last is not None and not any(arg is self.last for arg in args):
            args.append(self.last)
            in_specs.append(pl.BlockSpec(memory_space=pl.ANY))

            def placed(where, *refs, count=len(args) - 1):
                kernel(where, *refs[:count], *refs[count + 1 :])
        else:
            placed = kernel
        outs = pl.pallas_call(
            placed,
            grid_spec=pltpu.PrefetchScalarGridSpec(
                num_scalar_prefetch=1,
                grid=grid,
                in_specs=in_specs,
                out_specs=out_specs,
                scratch_shapes=scratch,
            ),
            out_shape=out_shape,
            input_output_aliases={i + 1: o for i, o in (aliases or {}).items()},
            cost_estimate=pl.CostEstimate(flops=cost[0], bytes_accessed=cost[1], transcendentals=0),
        )(self.where, *args)
        self.last = outs[-1]
        return outs


def prepare(plan, got):
    features = got.shape[2]
    half, share, slots = plan.group_features, plan.share, plan.slots

    def kernel(where, got_ref, own_ref, rows_ref, wide_ref):
        place, group = where[0] % plan.size, where[0] // plan.size
        for b in range(plan.dp_count):
            value = got_ref[b].astype(F32)
            for i in range(3):
                wide_ref[b * CAP : (b + 1) * CAP, i * features : (i + 1) * features] = value[
                    i * CAP : (i + 1) * CAP
                ]
        for i in range(2):
            own_ref[i] = wide_ref[:, i * features : (i + 1) * features].astype(BF)
            for k in range(plan.size):
                into = slice(k * share, (k + 1) * share)
                shift = (place ^ k) * share
                for p, base in ((0, i * features + group * half), (1, 2 * features + i * half)):
                    at = pl.multiple_of(base + shift, LANES)
                    rows_ref[2 * p + i, :, into] = wide_ref[:, pl.ds(at, share)].astype(BF)

    return plan.call(
        kernel,
        (1,),
        [full_spec(got.shape)],
        [got],
        [full_spec((2, slots, features)), full_spec((4, slots, half))],
        [
            jax.ShapeDtypeStruct((2, slots, features), BF),
            jax.ShapeDtypeStruct((4, slots, half), BF),
        ],
        (0, 4 * got.size),
        scratch=[pltpu.VMEM((slots, 3 * features), F32)],
    )


def pack(plan, up, down, start, width):
    step = plan.members * LANES
    first = start // step

    def kernel(where, *refs):
        del where
        sources, outs = refs[: plan.peers * 4], refs[-plan.peers :]
        for k in range(plan.peers):
            for i in range(4):
                outs[k][i] = sources[k * 4 + i][0]

    in_specs = [
        pl.BlockSpec(
            (1, plan.share, step),
            functools.partial(lambda i, where, p, k: (plan.part(where, p, k), 0, first + i), p=p, k=k),
        )
        for k in range(1, plan.size)
        for p in range(HALVES)
        for _ in range(2)
    ]
    return plan.call(
        kernel,
        (width // step,),
        in_specs,
        [up, down] * (plan.peers * HALVES),
        [
            pl.BlockSpec((4, plan.share, step), lambda i, where: (0, 0, i))
            for _ in range(plan.peers)
        ],
        [jax.ShapeDtypeStruct((4, plan.share, width), BF) for _ in range(plan.peers)],
        (0, plan.peers * 4 * plan.share * width * 4),
    )


def weight_specs(plan, start, width):
    own = pl.BlockSpec(
        (1, plan.share, width), lambda p, where: (plan.part(where, p), 0, start // width)
    )
    return [own, own] + [
        pl.BlockSpec((2, plan.share, width), lambda p, where: (p, 0, 0)) for _ in range(plan.peers)
    ]


def member_lanes(where, m, sub):
    return pl.ds(pl.multiple_of((where[1] ^ m) * sub, LANES), sub)


def stacked_rows(refs, i, lanes):
    return jnp.concatenate([refs[i][0, :, lanes]] + [ref[i, :, lanes] for ref in refs[2:]], axis=0)


def hidden_partials(plan, rows, up, down, came, start, width):
    sub = width // plan.members
    half, slots = plan.group_features, plan.slots

    def kernel(where, rows_ref, *refs):
        w_refs, outs = refs[: 2 + plan.peers], refs[-plan.members :]
        for m in range(plan.members):
            lanes = member_lanes(where, m, sub)
            for i in range(2):
                outs[m][i] = jnp.dot(
                    rows_ref[i], stacked_rows(w_refs, i, lanes), preferred_element_type=F32
                ).astype(BF)

    return plan.call(
        kernel,
        (HALVES,),
        [pl.BlockSpec((2, slots, half), lambda p, where: (p, 0, 0))]
        + weight_specs(plan, start, width),
        [rows, up, down, *came],
        [pl.BlockSpec((2, slots, sub), lambda p, where: (p, 0, 0)) for _ in range(plan.members)],
        [jax.ShapeDtypeStruct((4, slots, sub), BF) for _ in range(plan.members)],
        (8 * slots * half * width, 8 * width * (slots + half)),
    )


def sum_members(plan, parts):
    _, slots, sub = parts[0].shape

    def kernel(where, *refs):
        del where
        total = refs[0][...].astype(F32)
        for ref in refs[1 : plan.members]:
            total += ref[...].astype(F32)
        refs[-1][...] = total.astype(BF)

    spec = pl.BlockSpec((2, slots, sub), lambda p, where: (p, 0, 0))
    return plan.call(
        kernel,
        (HALVES,),
        [spec] * plan.members,
        parts,
        [spec],
        [jax.ShapeDtypeStruct((4, slots, sub), BF)],
        (0, 8 * slots * sub * (plan.members + 1)),
    )[0]


def activate(plan, sums, back):
    _, slots, sub = sums.shape

    def kernel(where, sums_ref, back_ref, *refs):
        del where
        pre, d_act = [sums_ref[i].astype(F32) + back_ref[i].astype(F32) for i in range(2)]
        sigma = 1.0 / (1.0 + jnp.exp(-pre))
        refs[-1][0] = (pre * sigma).astype(BF)
        refs[-1][1] = (d_act * sigma * (1.0 + pre * (1.0 - sigma))).astype(BF)

    spec = pl.BlockSpec((2, slots, sub), lambda p, where: (p, 0, 0))
    return plan.call(
        kernel,
        (HALVES,),
        [spec, pl.BlockSpec((2, slots, sub), lambda p, where: (1 - p, 0, 0))],
        [sums, back],
        [spec],
        [jax.ShapeDtypeStruct((4, slots, sub), BF)],
        (0, 24 * slots * sub),
    )[0]


def feature_sums(plan, total, pieces, up, down, came, start, width, final):
    sub = width // plan.members
    half, share, slots = plan.group_features, plan.share, plan.slots
    count = padded(4 * CAP)

    def kernel(where, *refs):
        place = where[0] % plan.size
        p_refs = refs[: plan.members]
        w_refs = refs[plan.members : plan.members + 2 + plan.peers]
        before = refs[plan.members + 2 + plan.peers]
        out, acc, wide = refs[-3:] if final else (refs[-1], None, None)
        for i in range(2):
            value = None
            for m in range(plan.members):
                weights = stacked_rows(w_refs, 1 - i, member_lanes(where, m, sub))
                term = contract(p_refs[m][i], weights, 1, 1)
                value = term if value is None else value + term
            for k in range(plan.size):
                at = pl.ds(pl.multiple_of((place ^ k) * share, LANES), share)
                piece = value[:, k * share : (k + 1) * share]
                if total is not None:
                    piece += before[i, :, at]
                if final:
                    acc[:, at] = piece
                else:
                    out[i, :, at] = piece
            if final:
                for p in range(HALVES):

                    @pl.when(pl.program_id(0) == p)
                    def _(first=(2 * p + i) * CAP):
                        for b in range(plan.dp_count):
                            wide[b, first : first + CAP, :] = acc[b * CAP : (b + 1) * CAP, :]

        if final:

            @pl.when(pl.program_id(0) == HALVES - 1)
            def _():
                for b in range(plan.dp_count):
                    if count > 4 * CAP:
                        wide[b, 4 * CAP :, :] = jnp.zeros((count - 4 * CAP, half), F32)
                    out[b] = wide[b].astype(BF)

    stack = pl.BlockSpec((2, slots, half), lambda p, where: (p, 0, 0))
    in_specs = [
        pl.BlockSpec((2, slots, sub), lambda p, where: (p, 0, 0)) for _ in range(plan.members)
    ] + weight_specs(plan, start, width)
    args = [*pieces, up, down, *came]
    if total is not None:
        in_specs.append(stack)
        args.append(total)
    if final:
        shape = (plan.dp_count, count, half)
        out_spec, out = full_spec(shape), jax.ShapeDtypeStruct(shape, BF)
        scratch = [pltpu.VMEM((slots, half), F32), pltpu.VMEM(shape, F32)]
    else:
        out_spec, out, scratch = stack, jax.ShapeDtypeStruct((4, slots, half), F32), ()
    return plan.call(
        kernel,
        (HALVES,),
        in_specs,
        args,
        [out_spec],
        [out],
        (8 * slots * half * width, 8 * width * (slots + half) + 32 * slots * half),
        scratch=scratch,
    )[0]


def weight_grads(plan, buffers, x_t, d_t, pieces, start, width):
    sub = width // plan.members
    features, slots = x_t.shape
    block = features // GRAD_STEPS

    def kernel(where, x_ref, d_ref, *refs):
        up_out, down_out = refs[-2:]
        for m in range(plan.members):
            lanes = member_lanes(where, m, sub)
            down_out[0, :, lanes] = jnp.dot(
                d_ref[...], refs[m][0], preferred_element_type=F32
            ).astype(BF)
            up_out[0, :, lanes] = jnp.dot(
                x_ref[...], refs[m][1], preferred_element_type=F32
            ).astype(BF)

    in_specs = [pl.BlockSpec((block, slots), lambda q, where: (q, 0))] * 2
    in_specs += [full_spec((2, slots, sub))] * plan.members
    args = [x_t, d_t, *pieces]
    aliases = {}
    if buffers is not None:
        aliases = {len(args): 0, len(args) + 1: 1}
        in_specs += [pl.BlockSpec(memory_space=pl.ANY)] * 2
        args += buffers
    return plan.call(
        kernel,
        (GRAD_STEPS,),
        in_specs,
        args,
        [pl.BlockSpec((1, block, width), lambda q, where: (0, q, start // width))] * 2,
        [jax.ShapeDtypeStruct((1, features, plan.hidden), BF) for _ in range(2)],
        (4 * features * slots * width, 4 * width * (slots + features)),
        aliases=aliases,
    )


def chunk_list(hidden, unit):
    units = hidden // unit
    wide = max(0, (units - 1) // 2)
    narrow = [(2 * wide + i, 1) for i in range(units - 2 * wide)]
    chunks = narrow[:-1] + [(2 * i, 2) for i in range(wide)] + narrow[-1:]
    return [(unit * start, unit * width) for start, width in chunks]


LAGS = (
    ("hidden", 0),
    ("features", 3),
    ("grads", 5),
    ("activate", 1),
    ("sums", 0),
    ("fetch", -2),
)


def order_of(count):
    steps = [("fetch", 0), ("route", 0), ("fetch", 1), ("prepare", 0)]
    for i in range(count + max(lag for _, lag in LAGS)):
        for kind, lag in LAGS:
            first = 2 if kind == "fetch" else 0
            if first <= i - lag < count:
                steps.append((kind, i - lag))
                if (kind, i - lag) == ("features", count - 1):
                    steps.append(("return", 0))
    return steps


def halves_body(tokens, routes, route_weights, up, down, cotangent):
    dp_count, members = lax.axis_size("dp"), lax.axis_size("member")
    share, hidden = up.shape[1:]
    plan = Plan(dp_count, members, share, hidden)

    chunks = chunk_list(hidden, members * LANES)
    count = len(chunks)
    routes_t, weights_t = routes.T, route_weights.T

    came, reduced, summed, backs, pieces = {}, {}, {}, {}, {}
    got = own = rows = total = grads = back = None
    for kind, i in order_of(count):
        if kind == "fetch":
            packed = pack(plan, up, down, *chunks[i])
        elif kind == "route":
            send = route(routes_t, weights_t, tokens, cotangent, dp_count)
        elif kind == "prepare":
            own, rows = prepare(plan, got)
        elif kind == "hidden":
            outs = hidden_partials(plan, rows, up, down, came[i], *chunks[i])
        elif kind == "sums":
            summed[i] = sum_members(plan, reduced[i])
        elif kind == "activate":
            acts = activate(plan, summed[i], backs[i])
        elif kind == "features":
            total = feature_sums(
                plan, total, pieces[i], up, down, came[i], *chunks[i], i == count - 1
            )
        elif kind == "grads":
            grads = weight_grads(plan, grads, x_t, d_t, pieces[i], *chunks[i])
        if kind == "fetch":
            came[i] = [plan.swap(packed[k], k + 1) for k in range(plan.peers)]
        elif kind == "route":
            got = lax.all_to_all(send, "dp", split_axis=0, concat_axis=0, tiled=True)
        elif kind == "prepare":
            x_t, d_t = own[0].T, own[1].T
        elif kind == "hidden":
            reduced[i] = [outs[0]] + [plan.pass_on(outs[k], k) for k in range(1, members)]
        elif kind == "sums":
            backs[i] = plan.swap(summed[i], plan.size)
        elif kind == "activate":
            pieces[i] = [acts] + [plan.pass_on(acts, k) for k in range(1, members)]
        elif kind == "return":
            back = lax.all_to_all(total, "dp", split_axis=0, concat_axis=0, tiled=True)

    out = jax.ShapeDtypeStruct(tokens.shape, BF)
    mixed, grad_tokens = pl.pallas_call(mix_kernel, out_shape=(out, out), name="mix")(
        routes_t, route_weights, back
    )
    return (mixed, grad_tokens, *grads)


def power_of_two(value):
    return value & (value - 1) == 0


def solution(mesh):
    placed = (
        P("dp", "member"),
        P("dp", None),
        P("dp", None),
        P(None, ("member", "dp"), None),
        P(None, ("member", "dp"), None),
        P("dp", "member"),
    )

    dp_count, members = mesh.shape["dp"], mesh.shape["member"]
    fits = (
        dp_count == E
        and power_of_two(members)
        and FF_W % (members * LANES) == 0
    )

    def body(*args):
        if not fits or args[3].shape[1] % LANES:
            return plain_body(*args)
        return halves_body(*args)

    return jax.shard_map(
        body,
        mesh=mesh,
        in_specs=placed,
        out_specs=(
            P("dp", "member"),
            P("dp", "member"),
            P("dp", "member", None),
            P("dp", "member", None),
        ),
        check_vma=False,
    )
```

```python
import functools

import jax
import jax.numpy as jnp
from jax import lax
from jax.experimental import pallas as pl
from jax.experimental.pallas import tpu as pltpu
from jax.sharding import PartitionSpec as P


FF_W = 7168
E = 8
CAP = 34
HALVES = 2
GRAD_STEPS = 4
LANES = 128
SUBLANES = 8
NOWHERE = -1e6
BF = jnp.bfloat16
F32 = jnp.float32


def contract(left, right, left_dim, right_dim):
    return lax.dot_general(
        left, right, (((left_dim,), (right_dim,)), ((), ())), preferred_element_type=jnp.float32
    )


def plain_body(tokens, routes, route_weights, up_stacked, down_stacked, cotangent):
    dp_count = lax.axis_size("dp")
    member_count = lax.axis_size("member")
    quarters = dp_count // E
    share_rows = up_stacked.shape[1]
    features = tokens.shape[1]
    hidden_own = FF_W // quarters
    per_member = hidden_own // member_count
    slots_all = E * CAP
    up_parts = (
        up_stacked.reshape(E, share_rows, quarters, hidden_own)
        .transpose(0, 2, 1, 3)
        .reshape(dp_count, share_rows, hidden_own)
    )
    down_parts = (
        down_stacked.reshape(E, share_rows, quarters, hidden_own)
        .transpose(0, 2, 1, 3)
        .reshape(dp_count, share_rows, hidden_own)
    )
    up_own, down_own = (
        lax.all_to_all(up_parts, "dp", split_axis=0, concat_axis=1, tiled=True),
        lax.all_to_all(down_parts, "dp", split_axis=0, concat_axis=1, tiled=True),
    )
    up_own = up_own.reshape(dp_count * share_rows, hidden_own)
    down_own = down_own.reshape(dp_count * share_rows, hidden_own)
    chosen = (routes[:, :, None] == jnp.arange(E, dtype=jnp.int32)[None, None, :]).astype(jnp.int32)
    flat_hits = chosen.reshape(-1, E)
    before = jnp.cumsum(flat_hits, axis=0) - flat_hits
    slot_pos = jnp.sum(before * flat_hits, axis=1).reshape(-1, 2)
    target = routes * CAP + slot_pos
    slot_hits = jnp.arange(slots_all, dtype=jnp.int32)[:, None, None] == target[None, :, :]
    pick_table = jnp.sum(slot_hits.astype(jnp.float32), axis=2)
    weighted = jnp.sum(jnp.where(slot_hits, route_weights[None, :, :], 0.0), axis=2)
    x_local = jnp.dot(
        pick_table.astype(jnp.bfloat16), tokens, preferred_element_type=jnp.float32
    ).astype(jnp.bfloat16)
    d_local = jnp.dot(
        weighted, cotangent.astype(jnp.float32), precision=lax.Precision.HIGHEST
    ).astype(jnp.bfloat16)

    def spread(local):
        return jnp.broadcast_to(
            local.reshape(E, 1, CAP, features), (E, quarters, CAP, features)
        ).reshape(dp_count, CAP, features)

    def collect(returned):
        return jnp.sum(returned.reshape(E, quarters, CAP, features), axis=1).reshape(
            slots_all, features
        )

    x_in = lax.all_to_all(spread(x_local), "dp", split_axis=0, concat_axis=0, tiled=True).reshape(
        dp_count * CAP, features
    )
    partial_value = jnp.dot(x_in, up_own, preferred_element_type=jnp.float32).astype(jnp.bfloat16)
    pre_full = lax.psum(partial_value, "member").astype(jnp.float32)
    act_full = jax.nn.silu(pre_full).astype(jnp.bfloat16)
    y_part = contract(act_full, down_own, 1, 1)
    y_back = lax.all_to_all(
        y_part.reshape(dp_count, CAP, features).astype(jnp.bfloat16),
        "dp",
        split_axis=0,
        concat_axis=0,
        tiled=True,
    ).astype(jnp.float32)
    d_in = lax.all_to_all(spread(d_local), "dp", split_axis=0, concat_axis=0, tiled=True).reshape(
        dp_count * CAP, features
    )
    d_act = lax.psum_scatter(
        contract(down_own, d_in, 0, 1).astype(jnp.bfloat16),
        "member",
        scatter_dimension=0,
        tiled=True,
    ).astype(jnp.float32)
    own_start = lax.axis_index("member") * per_member
    pre_share = lax.dynamic_slice_in_dim(pre_full, own_start, per_member, 1).T
    sigma = jax.nn.sigmoid(pre_share)
    d_share = (d_act * sigma * (1.0 + pre_share * (1.0 - sigma))).astype(jnp.bfloat16)
    d_pre = lax.all_gather(d_share, "member", axis=0, tiled=True)
    g_down = contract(d_in, act_full, 0, 0)
    g_up = contract(x_in, d_pre, 0, 1)
    dx_part = contract(d_pre, up_own, 0, 1)
    dx_back = lax.all_to_all(
        dx_part.reshape(dp_count, CAP, features).astype(jnp.bfloat16),
        "dp",
        split_axis=0,
        concat_axis=0,
        tiled=True,
    ).astype(jnp.float32)
    y_slots = collect(y_back)
    dx_slots = collect(dx_back)
    mixed = jnp.dot(weighted.T, y_slots, precision=lax.Precision.HIGHEST).astype(jnp.bfloat16)
    grad_tokens = jnp.dot(pick_table.T, dx_slots, precision=lax.Precision.HIGHEST).astype(
        jnp.bfloat16
    )
    grad_up = g_up.astype(jnp.bfloat16).reshape(1, features, hidden_own)
    grad_down = g_down.astype(jnp.bfloat16).reshape(1, features, hidden_own)
    return (mixed, grad_tokens, grad_up, grad_down)


def slot_rows(routes_ref):
    tok = routes_ref.shape[1]
    expert = lax.broadcasted_iota(jnp.int32, (E, tok), 0)
    hits = [(routes_ref[k : k + 1, :] == expert) for k in range(2)]
    either = jnp.where(hits[0] | hits[1], 1.0, 0.0).astype(BF)
    earlier = lax.broadcasted_iota(jnp.int32, (tok, tok), 0) < lax.broadcasted_iota(
        jnp.int32, (tok, tok), 1
    )
    before = jnp.dot(either, jnp.where(earlier, 1.0, 0.0).astype(BF), preferred_element_type=F32)
    return [jnp.where(hit, before, NOWHERE) for hit in hits]


def padded(rows):
    return -(-rows // SUBLANES) * SUBLANES


def slot_hits(rows, e, count=CAP, base=0):
    slot = lax.broadcasted_iota(jnp.int32, (count, rows[0].shape[1]), 0).astype(F32)
    return [jnp.where(slot == rows[k][e : e + 1, :] + base, 1.0, 0.0) for k in range(2)]


def route_kernel(routes_ref, weights_ref, tokens_ref, cot_ref, out_ref, wide_ref):
    features = tokens_ref.shape[1]
    size = out_ref.shape[0] // HALVES
    half = features // HALVES
    rows = slot_rows(routes_ref)
    for e in range(E):
        at = slot_hits(rows, e)
        pick = (at[0] + at[1]).astype(BF)
        scale = jnp.sum(at[0] * weights_ref[0:1, :] + at[1] * weights_ref[1:2, :], 1, keepdims=True)
        x_rows = jnp.dot(pick, tokens_ref[...], preferred_element_type=F32)
        d_rows = scale * jnp.dot(pick, cot_ref[...], preferred_element_type=F32)
        other = e ^ size
        cut = (other // size) * half
        for i, value in enumerate((x_rows, d_rows)):
            wide_ref[e, i * CAP : (i + 1) * CAP, :] = value
            wide_ref[other, 2 * CAP : 3 * CAP, i * half : (i + 1) * half] = value[:, cut : cut + half]
    extra = out_ref.shape[1] - 3 * CAP
    for e in range(E):
        if extra:
            wide_ref[e, 3 * CAP :, :] = jnp.zeros((extra, features), F32)
        out_ref[e] = wide_ref[e].astype(BF)


def route(routes_t, weights_t, tokens, cotangent, dp_count):
    features = tokens.shape[1]
    return pl.pallas_call(
        route_kernel,
        out_shape=jax.ShapeDtypeStruct((dp_count, padded(3 * CAP), features), BF),
        scratch_shapes=[pltpu.VMEM((dp_count, padded(3 * CAP), features), F32)],
        cost_estimate=pl.CostEstimate(
            flops=4 * E * CAP * tokens.size, bytes_accessed=2 * 10 * tokens.size, transcendentals=0
        ),
        name="route",
    )(routes_t, weights_t, tokens, cotangent)


def returned(size, e, half, kind):
    near = e // size == half
    return (e if near else e ^ size), (kind if near else 2 + kind) * CAP


def mix_kernel(routes_ref, weights_ref, back_ref, mixed_ref, grad_ref):
    tok = routes_ref.shape[1]
    rows = slot_rows(routes_ref)
    owners, count, width = back_ref.shape
    for half in range(HALVES):
        first, second, grad = [jnp.zeros((tok, width), F32) for _ in range(3)]
        for e in range(E):
            owner, base = returned(owners // HALVES, e, half, 0)
            at = slot_hits(rows, e, count, base)
            first += contract(at[0].astype(BF), back_ref[owner], 0, 0)
            second += contract(at[1].astype(BF), back_ref[owner], 0, 0)
            owner, base = returned(owners // HALVES, e, half, 1)
            at = slot_hits(rows, e, count, base)
            grad += contract((at[0] + at[1]).astype(BF), back_ref[owner], 0, 0)
        lanes = slice(half * width, (half + 1) * width)
        mixed_ref[:, lanes] = (weights_ref[:, 0:1] * first + weights_ref[:, 1:2] * second).astype(BF)
        grad_ref[:, lanes] = grad.astype(BF)


def full_spec(shape):
    return pl.BlockSpec(shape, lambda q, where: (0,) * len(shape))


class Plan:
    def __init__(self, dp_count, members, share, hidden):
        self.dp_count, self.members, self.share, self.hidden = dp_count, members, share, hidden
        self.size = dp_count // HALVES
        self.peers = self.size - 1
        self.group_features = self.size * share
        self.slots = dp_count * CAP
        self.where = jnp.stack([lax.axis_index("dp"), lax.axis_index("member")]).astype(jnp.int32)
        self.last = None

    def part(self, where, p, k=0):
        return (where[0] ^ (p * self.size)) ^ k

    def swap(self, value, k):
        return lax.ppermute(value, "dp", [(i, i ^ k) for i in range(self.dp_count)])

    def pass_on(self, value, k):
        return lax.ppermute(value, "member", [(i, i ^ k) for i in range(self.members)])

    def call(self, kernel, grid, in_specs, args, out_specs, out_shape, cost, aliases=None, scratch=()):
        args, in_specs = list(args), list(in_specs)
        if self.last is not None and not any(arg is self.last for arg in args):
            args.append(self.last)
            in_specs.append(pl.BlockSpec(memory_space=pl.ANY))

            def placed(where, *refs, count=len(args) - 1):
                kernel(where, *refs[:count], *refs[count + 1 :])
        else:
            placed = kernel
        outs = pl.pallas_call(
            placed,
            grid_spec=pltpu.PrefetchScalarGridSpec(
                num_scalar_prefetch=1,
                grid=grid,
                in_specs=in_specs,
                out_specs=out_specs,
                scratch_shapes=scratch,
            ),
            out_shape=out_shape,
            input_output_aliases={i + 1: o for i, o in (aliases or {}).items()},
            cost_estimate=pl.CostEstimate(flops=cost[0], bytes_accessed=cost[1], transcendentals=0),
        )(self.where, *args)
        self.last = outs[-1]
        return outs


def prepare(plan, got):
    features = got.shape[2]
    half, share, slots = plan.group_features, plan.share, plan.slots

    def kernel(where, got_ref, own_ref, rows_ref, wide_ref):
        place, group = where[0] % plan.size, where[0] // plan.size
        for b in range(plan.dp_count):
            value = got_ref[b].astype(F32)
            for i in range(3):
                wide_ref[b * CAP : (b + 1) * CAP, i * features : (i + 1) * features] = value[
                    i * CAP : (i + 1) * CAP
                ]
        for i in range(2):
            own_ref[i] = wide_ref[:, i * features : (i + 1) * features].astype(BF)
            for k in range(plan.size):
                into = slice(k * share, (k + 1) * share)
                shift = (place ^ k) * share
                for p, base in ((0, i * features + group * half), (1, 2 * features + i * half)):
                    at = pl.multiple_of(base + shift, LANES)
                    rows_ref[2 * p + i, :, into] = wide_ref[:, pl.ds(at, share)].astype(BF)

    return plan.call(
        kernel,
        (1,),
        [full_spec(got.shape)],
        [got],
        [full_spec((2, slots, features)), full_spec((4, slots, half))],
        [
            jax.ShapeDtypeStruct((2, slots, features), BF),
            jax.ShapeDtypeStruct((4, slots, half), BF),
        ],
        (0, 4 * got.size),
        scratch=[pltpu.VMEM((slots, 3 * features), F32)],
    )


def pack(plan, up, down, start, width):
    step = plan.members * LANES
    first = start // step

    def kernel(where, *refs):
        del where
        sources, outs = refs[: plan.peers * 4], refs[-plan.peers :]
        for k in range(plan.peers):
            for i in range(4):
                outs[k][i] = sources[k * 4 + i][0]

    in_specs = [
        pl.BlockSpec(
            (1, plan.share, step),
            functools.partial(lambda i, where, p, k: (plan.part(where, p, k), 0, first + i), p=p, k=k),
        )
        for k in range(1, plan.size)
        for p in range(HALVES)
        for _ in range(2)
    ]
    return plan.call(
        kernel,
        (width // step,),
        in_specs,
        [up, down] * (plan.peers * HALVES),
        [
            pl.BlockSpec((4, plan.share, step), lambda i, where: (0, 0, i))
            for _ in range(plan.peers)
        ],
        [jax.ShapeDtypeStruct((4, plan.share, width), BF) for _ in range(plan.peers)],
        (0, plan.peers * 4 * plan.share * width * 4),
    )


def weight_specs(plan, start, width):
    own = pl.BlockSpec(
        (1, plan.share, width), lambda p, where: (plan.part(where, p), 0, start // width)
    )
    return [own, own] + [
        pl.BlockSpec((2, plan.share, width), lambda p, where: (p, 0, 0)) for _ in range(plan.peers)
    ]


def member_lanes(where, m, sub):
    return pl.ds(pl.multiple_of((where[1] ^ m) * sub, LANES), sub)


def stacked_rows(refs, i, lanes):
    return jnp.concatenate([refs[i][0, :, lanes]] + [ref[i, :, lanes] for ref in refs[2:]], axis=0)


def hidden_partials(plan, rows, up, down, came, start, width):
    sub = width // plan.members
    half, slots = plan.group_features, plan.slots

    def kernel(where, rows_ref, *refs):
        w_refs, outs = refs[: 2 + plan.peers], refs[-plan.members :]
        for m in range(plan.members):
            lanes = member_lanes(where, m, sub)
            for i in range(2):
                outs[m][i] = jnp.dot(
                    rows_ref[i], stacked_rows(w_refs, i, lanes), preferred_element_type=F32
                ).astype(BF)

    return plan.call(
        kernel,
        (HALVES,),
        [pl.BlockSpec((2, slots, half), lambda p, where: (p, 0, 0))]
        + weight_specs(plan, start, width),
        [rows, up, down, *came],
        [pl.BlockSpec((2, slots, sub), lambda p, where: (p, 0, 0)) for _ in range(plan.members)],
        [jax.ShapeDtypeStruct((4, slots, sub), BF) for _ in range(plan.members)],
        (8 * slots * half * width, 8 * width * (slots + half)),
    )


def sum_members(plan, parts):
    _, slots, sub = parts[0].shape

    def kernel(where, *refs):
        del where
        total = refs[0][...].astype(F32)
        for ref in refs[1 : plan.members]:
            total += ref[...].astype(F32)
        refs[-1][...] = total.astype(BF)

    spec = pl.BlockSpec((2, slots, sub), lambda p, where: (p, 0, 0))
    return plan.call(
        kernel,
        (HALVES,),
        [spec] * plan.members,
        parts,
        [spec],
        [jax.ShapeDtypeStruct((4, slots, sub), BF)],
        (0, 8 * slots * sub * (plan.members + 1)),
    )[0]


def activate(plan, sums, back):
    _, slots, sub = sums.shape

    def kernel(where, sums_ref, back_ref, *refs):
        del where
        pre, d_act = [sums_ref[i].astype(F32) + back_ref[i].astype(F32) for i in range(2)]
        sigma = 1.0 / (1.0 + jnp.exp(-pre))
        refs[-1][0] = (pre * sigma).astype(BF)
        refs[-1][1] = (d_act * sigma * (1.0 + pre * (1.0 - sigma))).astype(BF)

    spec = pl.BlockSpec((2, slots, sub), lambda p, where: (p, 0, 0))
    return plan.call(
        kernel,
        (HALVES,),
        [spec, pl.BlockSpec((2, slots, sub), lambda p, where: (1 - p, 0, 0))],
        [sums, back],
        [spec],
        [jax.ShapeDtypeStruct((4, slots, sub), BF)],
        (0, 24 * slots * sub),
    )[0]


def feature_sums(plan, total, pieces, up, down, came, start, width, final):
    sub = width // plan.members
    half, share, slots = plan.group_features, plan.share, plan.slots
    count = padded(4 * CAP)

    def kernel(where, *refs):
        place = where[0] % plan.size
        p_refs = refs[: plan.members]
        w_refs = refs[plan.members : plan.members + 2 + plan.peers]
        before = refs[plan.members + 2 + plan.peers]
        out, acc, wide = refs[-3:] if final else (refs[-1], None, None)
        for i in range(2):
            value = None
            for m in range(plan.members):
                weights = stacked_rows(w_refs, 1 - i, member_lanes(where, m, sub))
                term = contract(p_refs[m][i], weights, 1, 1)
                value = term if value is None else value + term
            for k in range(plan.size):
                at = pl.ds(pl.multiple_of((place ^ k) * share, LANES), share)
                piece = value[:, k * share : (k + 1) * share]
                if total is not None:
                    piece += before[i, :, at]
                if final:
                    acc[:, at] = piece
                else:
                    out[i, :, at] = piece
            if final:
                for p in range(HALVES):

                    @pl.when(pl.program_id(0) == p)
                    def _(first=(2 * p + i) * CAP):
                        for b in range(plan.dp_count):
                            wide[b, first : first + CAP, :] = acc[b * CAP : (b + 1) * CAP, :]

        if final:

            @pl.when(pl.program_id(0) == HALVES - 1)
            def _():
                for b in range(plan.dp_count):
                    if count > 4 * CAP:
                        wide[b, 4 * CAP :, :] = jnp.zeros((count - 4 * CAP, half), F32)
                    out[b] = wide[b].astype(BF)

    stack = pl.BlockSpec((2, slots, half), lambda p, where: (p, 0, 0))
    in_specs = [
        pl.BlockSpec((2, slots, sub), lambda p, where: (p, 0, 0)) for _ in range(plan.members)
    ] + weight_specs(plan, start, width)
    args = [*pieces, up, down, *came]
    if total is not None:
        in_specs.append(stack)
        args.append(total)
    if final:
        shape = (plan.dp_count, count, half)
        out_spec, out = full_spec(shape), jax.ShapeDtypeStruct(shape, BF)
        scratch = [pltpu.VMEM((slots, half), F32), pltpu.VMEM(shape, F32)]
    else:
        out_spec, out, scratch = stack, jax.ShapeDtypeStruct((4, slots, half), F32), ()
    return plan.call(
        kernel,
        (HALVES,),
        in_specs,
        args,
        [out_spec],
        [out],
        (8 * slots * half * width, 8 * width * (slots + half) + 32 * slots * half),
        scratch=scratch,
    )[0]


def weight_grads(plan, buffers, x_t, d_t, pieces, start, width):
    sub = width // plan.members
    features, slots = x_t.shape
    block = features // GRAD_STEPS

    def kernel(where, x_ref, d_ref, *refs):
        up_out, down_out = refs[-2:]
        for m in range(plan.members):
            lanes = member_lanes(where, m, sub)
            down_out[0, :, lanes] = jnp.dot(
                d_ref[...], refs[m][0], preferred_element_type=F32
            ).astype(BF)
            up_out[0, :, lanes] = jnp.dot(
                x_ref[...], refs[m][1], preferred_element_type=F32
            ).astype(BF)

    in_specs = [pl.BlockSpec((block, slots), lambda q, where: (q, 0))] * 2
    in_specs += [full_spec((2, slots, sub))] * plan.members
    args = [x_t, d_t, *pieces]
    aliases = {}
    if buffers is not None:
        aliases = {len(args): 0, len(args) + 1: 1}
        in_specs += [pl.BlockSpec(memory_space=pl.ANY)] * 2
        args += buffers
    return plan.call(
        kernel,
        (GRAD_STEPS,),
        in_specs,
        args,
        [pl.BlockSpec((1, block, width), lambda q, where: (0, q, start // width))] * 2,
        [jax.ShapeDtypeStruct((1, features, plan.hidden), BF) for _ in range(2)],
        (4 * features * slots * width, 4 * width * (slots + features)),
        aliases=aliases,
    )


def chunk_list(hidden, unit):
    units = hidden // unit
    wide = max(0, (units - 1) // 2)
    narrow = [(2 * wide + i, 1) for i in range(units - 2 * wide)]
    chunks = narrow[:-1] + [(2 * i, 2) for i in range(wide)] + narrow[-1:]
    return [(unit * start, unit * width) for start, width in chunks]


LAGS = (
    ("hidden", 0),
    ("features", 3),
    ("activate", 1),
    ("sums", 0),
    ("fetch", -2),
    ("grads", 3),
)


def order_of(count):
    steps = [("fetch", 0), ("route", 0), ("fetch", 1), ("prepare", 0)]
    for i in range(count + max(lag for _, lag in LAGS)):
        for kind, lag in LAGS:
            first = 2 if kind == "fetch" else 0
            if first <= i - lag < count and (kind != "grads" or i < count):
                steps.append((kind, i - lag))
    steps.append(("return", 0))
    return steps + [("grads", i) for i in range(count) if ("grads", i) not in steps]


def halves_body(tokens, routes, route_weights, up, down, cotangent):
    dp_count, members = lax.axis_size("dp"), lax.axis_size("member")
    share, hidden = up.shape[1:]
    plan = Plan(dp_count, members, share, hidden)

    chunks = chunk_list(hidden, members * LANES)
    count = len(chunks)
    routes_t, weights_t = routes.T, route_weights.T

    came, reduced, summed, backs, pieces = {}, {}, {}, {}, {}
    got = own = rows = total = grads = back = None
    for kind, i in order_of(count):
        if kind == "fetch":
            packed = pack(plan, up, down, *chunks[i])
        elif kind == "route":
            send = route(routes_t, weights_t, tokens, cotangent, dp_count)
        elif kind == "prepare":
            own, rows = prepare(plan, got)
        elif kind == "hidden":
            outs = hidden_partials(plan, rows, up, down, came[i], *chunks[i])
        elif kind == "sums":
            summed[i] = sum_members(plan, reduced[i])
        elif kind == "activate":
            acts = activate(plan, summed[i], backs[i])
        elif kind == "features":
            total = feature_sums(
                plan, total, pieces[i], up, down, came[i], *chunks[i], i == count - 1
            )
        elif kind == "grads":
            grads = weight_grads(plan, grads, x_t, d_t, pieces[i], *chunks[i])
        if kind == "fetch":
            came[i] = [plan.swap(packed[k], k + 1) for k in range(plan.peers)]
        elif kind == "route":
            got = lax.all_to_all(send, "dp", split_axis=0, concat_axis=0, tiled=True)
        elif kind == "prepare":
            x_t, d_t = own[0].T, own[1].T
        elif kind == "hidden":
            reduced[i] = [outs[0]] + [plan.pass_on(outs[k], k) for k in range(1, members)]
        elif kind == "sums":
            backs[i] = plan.swap(summed[i], plan.size)
        elif kind == "activate":
            pieces[i] = [acts] + [plan.pass_on(acts, k) for k in range(1, members)]
        elif kind == "return":
            back = lax.all_to_all(total, "dp", split_axis=0, concat_axis=0, tiled=True)

    out = jax.ShapeDtypeStruct(tokens.shape, BF)
    mixed, grad_tokens = pl.pallas_call(mix_kernel, out_shape=(out, out), name="mix")(
        routes_t, route_weights, back
    )
    return (mixed, grad_tokens, *grads)


def power_of_two(value):
    return value & (value - 1) == 0


def solution(mesh):
    placed = (
        P("dp", "member"),
        P("dp", None),
        P("dp", None),
        P(None, ("member", "dp"), None),
        P(None, ("member", "dp"), None),
        P("dp", "member"),
    )

    dp_count, members = mesh.shape["dp"], mesh.shape["member"]
    fits = (
        dp_count == E
        and power_of_two(members)
        and FF_W % (members * LANES) == 0
    )

    def body(*args):
        if not fits or args[3].shape[1] % LANES:
            return plain_body(*args)
        return halves_body(*args)

    return jax.shard_map(
        body,
        mesh=mesh,
        in_specs=placed,
        out_specs=(
            P("dp", "member"),
            P("dp", "member"),
            P("dp", "member", None),
            P("dp", "member", None),
        ),
        check_vma=False,
    )
```

```python
import functools

import jax
import jax.numpy as jnp
from jax import lax
from jax.experimental import pallas as pl
from jax.experimental.pallas import tpu as pltpu
from jax.sharding import PartitionSpec as P


FF_W = 7168
E = 8
CAP = 34
HALVES = 2
GRAD_STEPS = 4
KERNEL_VMEM = 51 << 20
LANES = 128
SUBLANES = 8
NOWHERE = -1e6
BF = jnp.bfloat16
F32 = jnp.float32


def contract(left, right, left_dim, right_dim):
    return lax.dot_general(
        left, right, (((left_dim,), (right_dim,)), ((), ())), preferred_element_type=jnp.float32
    )


def plain_body(tokens, routes, route_weights, up_stacked, down_stacked, cotangent):
    dp_count = lax.axis_size("dp")
    member_count = lax.axis_size("member")
    quarters = dp_count // E
    share_rows = up_stacked.shape[1]
    features = tokens.shape[1]
    hidden_own = FF_W // quarters
    per_member = hidden_own // member_count
    slots_all = E * CAP
    up_parts = (
        up_stacked.reshape(E, share_rows, quarters, hidden_own)
        .transpose(0, 2, 1, 3)
        .reshape(dp_count, share_rows, hidden_own)
    )
    down_parts = (
        down_stacked.reshape(E, share_rows, quarters, hidden_own)
        .transpose(0, 2, 1, 3)
        .reshape(dp_count, share_rows, hidden_own)
    )
    up_own, down_own = (
        lax.all_to_all(up_parts, "dp", split_axis=0, concat_axis=1, tiled=True),
        lax.all_to_all(down_parts, "dp", split_axis=0, concat_axis=1, tiled=True),
    )
    up_own = up_own.reshape(dp_count * share_rows, hidden_own)
    down_own = down_own.reshape(dp_count * share_rows, hidden_own)
    chosen = (routes[:, :, None] == jnp.arange(E, dtype=jnp.int32)[None, None, :]).astype(jnp.int32)
    flat_hits = chosen.reshape(-1, E)
    before = jnp.cumsum(flat_hits, axis=0) - flat_hits
    slot_pos = jnp.sum(before * flat_hits, axis=1).reshape(-1, 2)
    target = routes * CAP + slot_pos
    slot_hits = jnp.arange(slots_all, dtype=jnp.int32)[:, None, None] == target[None, :, :]
    pick_table = jnp.sum(slot_hits.astype(jnp.float32), axis=2)
    weighted = jnp.sum(jnp.where(slot_hits, route_weights[None, :, :], 0.0), axis=2)
    x_local = jnp.dot(
        pick_table.astype(jnp.bfloat16), tokens, preferred_element_type=jnp.float32
    ).astype(jnp.bfloat16)
    d_local = jnp.dot(
        weighted, cotangent.astype(jnp.float32), precision=lax.Precision.HIGHEST
    ).astype(jnp.bfloat16)

    def spread(local):
        return jnp.broadcast_to(
            local.reshape(E, 1, CAP, features), (E, quarters, CAP, features)
        ).reshape(dp_count, CAP, features)

    def collect(returned):
        return jnp.sum(returned.reshape(E, quarters, CAP, features), axis=1).reshape(
            slots_all, features
        )

    x_in = lax.all_to_all(spread(x_local), "dp", split_axis=0, concat_axis=0, tiled=True).reshape(
        dp_count * CAP, features
    )
    partial_value = jnp.dot(x_in, up_own, preferred_element_type=jnp.float32).astype(jnp.bfloat16)
    pre_full = lax.psum(partial_value, "member").astype(jnp.float32)
    act_full = jax.nn.silu(pre_full).astype(jnp.bfloat16)
    y_part = contract(act_full, down_own, 1, 1)
    y_back = lax.all_to_all(
        y_part.reshape(dp_count, CAP, features).astype(jnp.bfloat16),
        "dp",
        split_axis=0,
        concat_axis=0,
        tiled=True,
    ).astype(jnp.float32)
    d_in = lax.all_to_all(spread(d_local), "dp", split_axis=0, concat_axis=0, tiled=True).reshape(
        dp_count * CAP, features
    )
    d_act = lax.psum_scatter(
        contract(down_own, d_in, 0, 1).astype(jnp.bfloat16),
        "member",
        scatter_dimension=0,
        tiled=True,
    ).astype(jnp.float32)
    own_start = lax.axis_index("member") * per_member
    pre_share = lax.dynamic_slice_in_dim(pre_full, own_start, per_member, 1).T
    sigma = jax.nn.sigmoid(pre_share)
    d_share = (d_act * sigma * (1.0 + pre_share * (1.0 - sigma))).astype(jnp.bfloat16)
    d_pre = lax.all_gather(d_share, "member", axis=0, tiled=True)
    g_down = contract(d_in, act_full, 0, 0)
    g_up = contract(x_in, d_pre, 0, 1)
    dx_part = contract(d_pre, up_own, 0, 1)
    dx_back = lax.all_to_all(
        dx_part.reshape(dp_count, CAP, features).astype(jnp.bfloat16),
        "dp",
        split_axis=0,
        concat_axis=0,
        tiled=True,
    ).astype(jnp.float32)
    y_slots = collect(y_back)
    dx_slots = collect(dx_back)
    mixed = jnp.dot(weighted.T, y_slots, precision=lax.Precision.HIGHEST).astype(jnp.bfloat16)
    grad_tokens = jnp.dot(pick_table.T, dx_slots, precision=lax.Precision.HIGHEST).astype(
        jnp.bfloat16
    )
    grad_up = g_up.astype(jnp.bfloat16).reshape(1, features, hidden_own)
    grad_down = g_down.astype(jnp.bfloat16).reshape(1, features, hidden_own)
    return (mixed, grad_tokens, grad_up, grad_down)


def slot_rows(routes_ref):
    tok = routes_ref.shape[1]
    expert = lax.broadcasted_iota(jnp.int32, (E, tok), 0)
    hits = [(routes_ref[k : k + 1, :] == expert) for k in range(2)]
    either = jnp.where(hits[0] | hits[1], 1.0, 0.0).astype(BF)
    earlier = lax.broadcasted_iota(jnp.int32, (tok, tok), 0) < lax.broadcasted_iota(
        jnp.int32, (tok, tok), 1
    )
    before = jnp.dot(either, jnp.where(earlier, 1.0, 0.0).astype(BF), preferred_element_type=F32)
    return [jnp.where(hit, before, NOWHERE) for hit in hits]


def padded(rows):
    return -(-rows // SUBLANES) * SUBLANES


def slot_hits(rows, e, count=CAP, base=0):
    slot = lax.broadcasted_iota(jnp.int32, (count, rows[0].shape[1]), 0).astype(F32)
    return [jnp.where(slot == rows[k][e : e + 1, :] + base, 1.0, 0.0) for k in range(2)]


def route_kernel(routes_ref, weights_ref, tokens_ref, cot_ref, out_ref, wide_ref):
    features = tokens_ref.shape[1]
    size = out_ref.shape[0] // HALVES
    half = features // HALVES
    rows = slot_rows(routes_ref)
    for e in range(E):
        at = slot_hits(rows, e)
        pick = (at[0] + at[1]).astype(BF)
        scale = jnp.sum(at[0] * weights_ref[0:1, :] + at[1] * weights_ref[1:2, :], 1, keepdims=True)
        x_rows = jnp.dot(pick, tokens_ref[...], preferred_element_type=F32)
        d_rows = scale * jnp.dot(pick, cot_ref[...], preferred_element_type=F32)
        other = e ^ size
        cut = (other // size) * half
        for i, value in enumerate((x_rows, d_rows)):
            wide_ref[e, i * CAP : (i + 1) * CAP, :] = value
            wide_ref[other, 2 * CAP : 3 * CAP, i * half : (i + 1) * half] = value[:, cut : cut + half]
    extra = out_ref.shape[1] - 3 * CAP
    for e in range(E):
        if extra:
            wide_ref[e, 3 * CAP :, :] = jnp.zeros((extra, features), F32)
        out_ref[e] = wide_ref[e].astype(BF)


def route(routes_t, weights_t, tokens, cotangent, dp_count):
    features = tokens.shape[1]
    return pl.pallas_call(
        route_kernel,
        out_shape=jax.ShapeDtypeStruct((dp_count, padded(3 * CAP), features), BF),
        scratch_shapes=[pltpu.VMEM((dp_count, padded(3 * CAP), features), F32)],
        cost_estimate=pl.CostEstimate(
            flops=4 * E * CAP * tokens.size, bytes_accessed=2 * 10 * tokens.size, transcendentals=0
        ),
        compiler_params=pltpu.CompilerParams(vmem_limit_bytes=KERNEL_VMEM),
        name="route",
    )(routes_t, weights_t, tokens, cotangent)


def returned(size, e, half, kind):
    near = e // size == half
    return (e if near else e ^ size), (kind if near else 2 + kind) * CAP


def mix_kernel(routes_ref, weights_ref, back_ref, mixed_ref, grad_ref):
    tok = routes_ref.shape[1]
    rows = slot_rows(routes_ref)
    owners, count, width = back_ref.shape
    for half in range(HALVES):
        first, second, grad = [jnp.zeros((tok, width), F32) for _ in range(3)]
        for e in range(E):
            owner, base = returned(owners // HALVES, e, half, 0)
            at = slot_hits(rows, e, count, base)
            first += contract(at[0].astype(BF), back_ref[owner], 0, 0)
            second += contract(at[1].astype(BF), back_ref[owner], 0, 0)
            owner, base = returned(owners // HALVES, e, half, 1)
            at = slot_hits(rows, e, count, base)
            grad += contract((at[0] + at[1]).astype(BF), back_ref[owner], 0, 0)
        lanes = slice(half * width, (half + 1) * width)
        mixed_ref[:, lanes] = (weights_ref[:, 0:1] * first + weights_ref[:, 1:2] * second).astype(BF)
        grad_ref[:, lanes] = grad.astype(BF)


def full_spec(shape):
    return pl.BlockSpec(shape, lambda q, where: (0,) * len(shape))


class Plan:
    def __init__(self, dp_count, members, share, hidden):
        self.dp_count, self.members, self.share, self.hidden = dp_count, members, share, hidden
        self.size = dp_count // HALVES
        self.peers = self.size - 1
        self.group_features = self.size * share
        self.slots = dp_count * CAP
        self.where = jnp.stack([lax.axis_index("dp"), lax.axis_index("member")]).astype(jnp.int32)
        self.last = None

    def part(self, where, p, k=0):
        return (where[0] ^ (p * self.size)) ^ k

    def swap(self, value, k):
        return lax.ppermute(value, "dp", [(i, i ^ k) for i in range(self.dp_count)])

    def pass_on(self, value, k):
        return lax.ppermute(value, "member", [(i, i ^ k) for i in range(self.members)])

    def call(self, kernel, grid, in_specs, args, out_specs, out_shape, cost, aliases=None, scratch=()):
        args, in_specs = list(args), list(in_specs)
        if self.last is not None and not any(arg is self.last for arg in args):
            args.append(self.last)
            in_specs.append(pl.BlockSpec(memory_space=pl.ANY))

            def placed(where, *refs, count=len(args) - 1):
                kernel(where, *refs[:count], *refs[count + 1 :])
        else:
            placed = kernel
        outs = pl.pallas_call(
            placed,
            grid_spec=pltpu.PrefetchScalarGridSpec(
                num_scalar_prefetch=1,
                grid=grid,
                in_specs=in_specs,
                out_specs=out_specs,
                scratch_shapes=scratch,
            ),
            out_shape=out_shape,
            input_output_aliases={i + 1: o for i, o in (aliases or {}).items()},
            cost_estimate=pl.CostEstimate(flops=cost[0], bytes_accessed=cost[1], transcendentals=0),
            compiler_params=pltpu.CompilerParams(vmem_limit_bytes=KERNEL_VMEM),
        )(self.where, *args)
        self.last = outs[-1]
        return outs


def prepare(plan, got):
    features = got.shape[2]
    half, share, slots = plan.group_features, plan.share, plan.slots

    def kernel(where, got_ref, own_ref, rows_ref, wide_ref):
        place, group = where[0] % plan.size, where[0] // plan.size
        for b in range(plan.dp_count):
            value = got_ref[b].astype(F32)
            for i in range(3):
                wide_ref[b * CAP : (b + 1) * CAP, i * features : (i + 1) * features] = value[
                    i * CAP : (i + 1) * CAP
                ]
        for i in range(2):
            own_ref[i] = wide_ref[:, i * features : (i + 1) * features].astype(BF)
            for k in range(plan.size):
                into = slice(k * share, (k + 1) * share)
                shift = (place ^ k) * share
                for p, base in ((0, i * features + group * half), (1, 2 * features + i * half)):
                    at = pl.multiple_of(base + shift, LANES)
                    rows_ref[2 * p + i, :, into] = wide_ref[:, pl.ds(at, share)].astype(BF)

    return plan.call(
        kernel,
        (1,),
        [full_spec(got.shape)],
        [got],
        [full_spec((2, slots, features)), full_spec((4, slots, half))],
        [
            jax.ShapeDtypeStruct((2, slots, features), BF),
            jax.ShapeDtypeStruct((4, slots, half), BF),
        ],
        (0, 4 * got.size),
        scratch=[pltpu.VMEM((slots, 3 * features), F32)],
    )


def pack(plan, up, down, start, width):
    step = plan.members * LANES
    first = start // step

    def kernel(where, *refs):
        del where
        sources, outs = refs[: plan.peers * 4], refs[-plan.peers :]
        for k in range(plan.peers):
            for i in range(4):
                outs[k][i] = sources[k * 4 + i][0]

    in_specs = [
        pl.BlockSpec(
            (1, plan.share, step),
            functools.partial(lambda i, where, p, k: (plan.part(where, p, k), 0, first + i), p=p, k=k),
        )
        for k in range(1, plan.size)
        for p in range(HALVES)
        for _ in range(2)
    ]
    return plan.call(
        kernel,
        (width // step,),
        in_specs,
        [up, down] * (plan.peers * HALVES),
        [
            pl.BlockSpec((4, plan.share, step), lambda i, where: (0, 0, i))
            for _ in range(plan.peers)
        ],
        [jax.ShapeDtypeStruct((4, plan.share, width), BF) for _ in range(plan.peers)],
        (0, plan.peers * 4 * plan.share * width * 4),
    )


def weight_specs(plan, start, width):
    own = pl.BlockSpec(
        (1, plan.share, width), lambda p, where: (plan.part(where, p), 0, start // width)
    )
    return [own, own] + [
        pl.BlockSpec((2, plan.share, width), lambda p, where: (p, 0, 0)) for _ in range(plan.peers)
    ]


def member_lanes(where, m, sub):
    return pl.ds(pl.multiple_of((where[1] ^ m) * sub, LANES), sub)


def stacked_rows(refs, i, lanes):
    return jnp.concatenate([refs[i][0, :, lanes]] + [ref[i, :, lanes] for ref in refs[2:]], axis=0)


def hidden_partials(plan, rows, up, down, came, start, width):
    sub = width // plan.members
    half, slots = plan.group_features, plan.slots

    def kernel(where, rows_ref, *refs):
        w_refs, outs = refs[: 2 + plan.peers], refs[-plan.members :]
        for m in range(plan.members):
            lanes = member_lanes(where, m, sub)
            for i in range(2):
                outs[m][i] = jnp.dot(
                    rows_ref[i], stacked_rows(w_refs, i, lanes), preferred_element_type=F32
                ).astype(BF)

    return plan.call(
        kernel,
        (HALVES,),
        [pl.BlockSpec((2, slots, half), lambda p, where: (p, 0, 0))]
        + weight_specs(plan, start, width),
        [rows, up, down, *came],
        [pl.BlockSpec((2, slots, sub), lambda p, where: (p, 0, 0)) for _ in range(plan.members)],
        [jax.ShapeDtypeStruct((4, slots, sub), BF) for _ in range(plan.members)],
        (8 * slots * half * width, 8 * width * (slots + half)),
    )


def sum_members(plan, parts):
    _, slots, sub = parts[0].shape

    def kernel(where, *refs):
        del where
        total = refs[0][...].astype(F32)
        for ref in refs[1 : plan.members]:
            total += ref[...].astype(F32)
        refs[-1][...] = total.astype(BF)

    spec = pl.BlockSpec((2, slots, sub), lambda p, where: (p, 0, 0))
    return plan.call(
        kernel,
        (HALVES,),
        [spec] * plan.members,
        parts,
        [spec],
        [jax.ShapeDtypeStruct((4, slots, sub), BF)],
        (0, 8 * slots * sub * (plan.members + 1)),
    )[0]


def activate(plan, sums, back):
    _, slots, sub = sums.shape

    def kernel(where, sums_ref, back_ref, *refs):
        del where
        pre, d_act = [sums_ref[i].astype(F32) + back_ref[i].astype(F32) for i in range(2)]
        sigma = 1.0 / (1.0 + jnp.exp(-pre))
        refs[-1][0] = (pre * sigma).astype(BF)
        refs[-1][1] = (d_act * sigma * (1.0 + pre * (1.0 - sigma))).astype(BF)

    spec = pl.BlockSpec((2, slots, sub), lambda p, where: (p, 0, 0))
    return plan.call(
        kernel,
        (HALVES,),
        [spec, pl.BlockSpec((2, slots, sub), lambda p, where: (1 - p, 0, 0))],
        [sums, back],
        [spec],
        [jax.ShapeDtypeStruct((4, slots, sub), BF)],
        (0, 24 * slots * sub),
    )[0]


def feature_sums(plan, total, pieces, up, down, came, start, width, final):
    sub = width // plan.members
    half, share, slots = plan.group_features, plan.share, plan.slots
    count = padded(4 * CAP)

    def kernel(where, *refs):
        place = where[0] % plan.size
        p_refs = refs[: plan.members]
        w_refs = refs[plan.members : plan.members + 2 + plan.peers]
        before = refs[plan.members + 2 + plan.peers]
        out, acc, wide = refs[-3:] if final else (refs[-1], None, None)
        for i in range(2):
            value = None
            for m in range(plan.members):
                weights = stacked_rows(w_refs, 1 - i, member_lanes(where, m, sub))
                term = contract(p_refs[m][i], weights, 1, 1)
                value = term if value is None else value + term
            for k in range(plan.size):
                at = pl.ds(pl.multiple_of((place ^ k) * share, LANES), share)
                piece = value[:, k * share : (k + 1) * share]
                if total is not None:
                    piece += before[i, :, at]
                if final:
                    acc[:, at] = piece
                else:
                    out[i, :, at] = piece
            if final:
                for p in range(HALVES):

                    @pl.when(pl.program_id(0) == p)
                    def _(first=(2 * p + i) * CAP):
                        for b in range(plan.dp_count):
                            wide[b, first : first + CAP, :] = acc[b * CAP : (b + 1) * CAP, :]

        if final:

            @pl.when(pl.program_id(0) == HALVES - 1)
            def _():
                for b in range(plan.dp_count):
                    if count > 4 * CAP:
                        wide[b, 4 * CAP :, :] = jnp.zeros((count - 4 * CAP, half), F32)
                    out[b] = wide[b].astype(BF)

    stack = pl.BlockSpec((2, slots, half), lambda p, where: (p, 0, 0))
    in_specs = [
        pl.BlockSpec((2, slots, sub), lambda p, where: (p, 0, 0)) for _ in range(plan.members)
    ] + weight_specs(plan, start, width)
    args = [*pieces, up, down, *came]
    if total is not None:
        in_specs.append(stack)
        args.append(total)
    if final:
        shape = (plan.dp_count, count, half)
        out_spec, out = full_spec(shape), jax.ShapeDtypeStruct(shape, BF)
        scratch = [pltpu.VMEM((slots, half), F32), pltpu.VMEM(shape, F32)]
    else:
        out_spec, out, scratch = stack, jax.ShapeDtypeStruct((4, slots, half), F32), ()
    return plan.call(
        kernel,
        (HALVES,),
        in_specs,
        args,
        [out_spec],
        [out],
        (8 * slots * half * width, 8 * width * (slots + half) + 32 * slots * half),
        scratch=scratch,
    )[0]


def weight_grads(plan, buffers, x_t, d_t, pieces, start, width):
    sub = width // plan.members
    features, slots = x_t.shape
    block = features // GRAD_STEPS

    def kernel(where, x_ref, d_ref, *refs):
        up_out, down_out = refs[-2:]
        for m in range(plan.members):
            lanes = member_lanes(where, m, sub)
            down_out[0, :, lanes] = jnp.dot(
                d_ref[...], refs[m][0], preferred_element_type=F32
            ).astype(BF)
            up_out[0, :, lanes] = jnp.dot(
                x_ref[...], refs[m][1], preferred_element_type=F32
            ).astype(BF)

    in_specs = [pl.BlockSpec((block, slots), lambda q, where: (q, 0))] * 2
    in_specs += [full_spec((2, slots, sub))] * plan.members
    args = [x_t, d_t, *pieces]
    aliases = {}
    if buffers is not None:
        aliases = {len(args): 0, len(args) + 1: 1}
        in_specs += [pl.BlockSpec(memory_space=pl.ANY)] * 2
        args += buffers
    return plan.call(
        kernel,
        (GRAD_STEPS,),
        in_specs,
        args,
        [pl.BlockSpec((1, block, width), lambda q, where: (0, q, start // width))] * 2,
        [jax.ShapeDtypeStruct((1, features, plan.hidden), BF) for _ in range(2)],
        (4 * features * slots * width, 4 * width * (slots + features)),
        aliases=aliases,
    )


def chunk_list(hidden, unit):
    units = hidden // unit
    wide = max(0, (units - 1) // 2)
    narrow = [(2 * wide + i, 1) for i in range(units - 2 * wide)]
    chunks = narrow[:-1] + [(2 * i, 2) for i in range(wide)] + narrow[-1:]
    return [(unit * start, unit * width) for start, width in chunks]


LAGS = (
    ("hidden", 0),
    ("features", 3),
    ("activate", 1),
    ("sums", 0),
    ("fetch", -2),
    ("grads", 3),
)


def order_of(count):
    steps = [("fetch", 0), ("route", 0), ("fetch", 1), ("prepare", 0)]
    for i in range(count + max(lag for _, lag in LAGS)):
        for kind, lag in LAGS:
            first = 2 if kind == "fetch" else 0
            if first <= i - lag < count and (kind != "grads" or i < count):
                steps.append((kind, i - lag))
    steps.append(("return", 0))
    return steps + [("grads", i) for i in range(count) if ("grads", i) not in steps]


def halves_body(tokens, routes, route_weights, up, down, cotangent):
    dp_count, members = lax.axis_size("dp"), lax.axis_size("member")
    share, hidden = up.shape[1:]
    plan = Plan(dp_count, members, share, hidden)

    chunks = chunk_list(hidden, members * LANES)
    count = len(chunks)
    routes_t, weights_t = routes.T, route_weights.T

    came, reduced, summed, backs, pieces = {}, {}, {}, {}, {}
    got = own = rows = total = grads = back = None
    for kind, i in order_of(count):
        if kind == "fetch":
            packed = pack(plan, up, down, *chunks[i])
        elif kind == "route":
            send = route(routes_t, weights_t, tokens, cotangent, dp_count)
        elif kind == "prepare":
            own, rows = prepare(plan, got)
        elif kind == "hidden":
            outs = hidden_partials(plan, rows, up, down, came[i], *chunks[i])
        elif kind == "sums":
            summed[i] = sum_members(plan, reduced[i])
        elif kind == "activate":
            acts = activate(plan, summed[i], backs[i])
        elif kind == "features":
            total = feature_sums(
                plan, total, pieces[i], up, down, came[i], *chunks[i], i == count - 1
            )
        elif kind == "grads":
            grads = weight_grads(plan, grads, x_t, d_t, pieces[i], *chunks[i])
        if kind == "fetch":
            came[i] = [plan.swap(packed[k], k + 1) for k in range(plan.peers)]
        elif kind == "route":
            got = lax.all_to_all(send, "dp", split_axis=0, concat_axis=0, tiled=True)
        elif kind == "prepare":
            x_t, d_t = own[0].T, own[1].T
        elif kind == "hidden":
            reduced[i] = [outs[0]] + [plan.pass_on(outs[k], k) for k in range(1, members)]
        elif kind == "sums":
            backs[i] = plan.swap(summed[i], plan.size)
        elif kind == "activate":
            pieces[i] = [acts] + [plan.pass_on(acts, k) for k in range(1, members)]
        elif kind == "return":
            back = lax.all_to_all(total, "dp", split_axis=0, concat_axis=0, tiled=True)

    out = jax.ShapeDtypeStruct(tokens.shape, BF)
    mixed, grad_tokens = pl.pallas_call(
        mix_kernel,
        out_shape=(out, out),
        compiler_params=pltpu.CompilerParams(vmem_limit_bytes=KERNEL_VMEM),
        name="mix",
    )(routes_t, route_weights, back)
    return (mixed, grad_tokens, *grads)


def power_of_two(value):
    return value & (value - 1) == 0


def solution(mesh):
    placed = (
        P("dp", "member"),
        P("dp", None),
        P("dp", None),
        P(None, ("member", "dp"), None),
        P(None, ("member", "dp"), None),
        P("dp", "member"),
    )

    dp_count, members = mesh.shape["dp"], mesh.shape["member"]
    fits = (
        dp_count == E
        and power_of_two(members)
        and FF_W % (members * LANES) == 0
    )

    def body(*args):
        if not fits or args[3].shape[1] % LANES:
            return plain_body(*args)
        return halves_body(*args)

    return jax.shard_map(
        body,
        mesh=mesh,
        in_specs=placed,
        out_specs=(
            P("dp", "member"),
            P("dp", "member"),
            P("dp", "member", None),
            P("dp", "member", None),
        ),
        check_vma=False,
    )
```

```python
import functools

import jax
import jax.numpy as jnp
from jax import lax
from jax.experimental import pallas as pl
from jax.experimental.pallas import tpu as pltpu
from jax.sharding import PartitionSpec as P


FF_W = 7168
E = 8
CAP = 34
HALVES = 2
GRAD_STEPS = 8
KERNEL_VMEM = 51 << 20
LANES = 128
SUBLANES = 8
NOWHERE = -1e6
BF = jnp.bfloat16
F32 = jnp.float32


def contract(left, right, left_dim, right_dim):
    return lax.dot_general(
        left, right, (((left_dim,), (right_dim,)), ((), ())), preferred_element_type=jnp.float32
    )


def plain_body(tokens, routes, route_weights, up_stacked, down_stacked, cotangent):
    dp_count = lax.axis_size("dp")
    member_count = lax.axis_size("member")
    quarters = dp_count // E
    share_rows = up_stacked.shape[1]
    features = tokens.shape[1]
    hidden_own = FF_W // quarters
    per_member = hidden_own // member_count
    slots_all = E * CAP
    up_parts = (
        up_stacked.reshape(E, share_rows, quarters, hidden_own)
        .transpose(0, 2, 1, 3)
        .reshape(dp_count, share_rows, hidden_own)
    )
    down_parts = (
        down_stacked.reshape(E, share_rows, quarters, hidden_own)
        .transpose(0, 2, 1, 3)
        .reshape(dp_count, share_rows, hidden_own)
    )
    up_own, down_own = (
        lax.all_to_all(up_parts, "dp", split_axis=0, concat_axis=1, tiled=True),
        lax.all_to_all(down_parts, "dp", split_axis=0, concat_axis=1, tiled=True),
    )
    up_own = up_own.reshape(dp_count * share_rows, hidden_own)
    down_own = down_own.reshape(dp_count * share_rows, hidden_own)
    chosen = (routes[:, :, None] == jnp.arange(E, dtype=jnp.int32)[None, None, :]).astype(jnp.int32)
    flat_hits = chosen.reshape(-1, E)
    before = jnp.cumsum(flat_hits, axis=0) - flat_hits
    slot_pos = jnp.sum(before * flat_hits, axis=1).reshape(-1, 2)
    target = routes * CAP + slot_pos
    slot_hits = jnp.arange(slots_all, dtype=jnp.int32)[:, None, None] == target[None, :, :]
    pick_table = jnp.sum(slot_hits.astype(jnp.float32), axis=2)
    weighted = jnp.sum(jnp.where(slot_hits, route_weights[None, :, :], 0.0), axis=2)
    x_local = jnp.dot(
        pick_table.astype(jnp.bfloat16), tokens, preferred_element_type=jnp.float32
    ).astype(jnp.bfloat16)
    d_local = jnp.dot(
        weighted, cotangent.astype(jnp.float32), precision=lax.Precision.HIGHEST
    ).astype(jnp.bfloat16)

    def spread(local):
        return jnp.broadcast_to(
            local.reshape(E, 1, CAP, features), (E, quarters, CAP, features)
        ).reshape(dp_count, CAP, features)

    def collect(returned):
        return jnp.sum(returned.reshape(E, quarters, CAP, features), axis=1).reshape(
            slots_all, features
        )

    x_in = lax.all_to_all(spread(x_local), "dp", split_axis=0, concat_axis=0, tiled=True).reshape(
        dp_count * CAP, features
    )
    partial_value = jnp.dot(x_in, up_own, preferred_element_type=jnp.float32).astype(jnp.bfloat16)
    pre_full = lax.psum(partial_value, "member").astype(jnp.float32)
    act_full = jax.nn.silu(pre_full).astype(jnp.bfloat16)
    y_part = contract(act_full, down_own, 1, 1)
    y_back = lax.all_to_all(
        y_part.reshape(dp_count, CAP, features).astype(jnp.bfloat16),
        "dp",
        split_axis=0,
        concat_axis=0,
        tiled=True,
    ).astype(jnp.float32)
    d_in = lax.all_to_all(spread(d_local), "dp", split_axis=0, concat_axis=0, tiled=True).reshape(
        dp_count * CAP, features
    )
    d_act = lax.psum_scatter(
        contract(down_own, d_in, 0, 1).astype(jnp.bfloat16),
        "member",
        scatter_dimension=0,
        tiled=True,
    ).astype(jnp.float32)
    own_start = lax.axis_index("member") * per_member
    pre_share = lax.dynamic_slice_in_dim(pre_full, own_start, per_member, 1).T
    sigma = jax.nn.sigmoid(pre_share)
    d_share = (d_act * sigma * (1.0 + pre_share * (1.0 - sigma))).astype(jnp.bfloat16)
    d_pre = lax.all_gather(d_share, "member", axis=0, tiled=True)
    g_down = contract(d_in, act_full, 0, 0)
    g_up = contract(x_in, d_pre, 0, 1)
    dx_part = contract(d_pre, up_own, 0, 1)
    dx_back = lax.all_to_all(
        dx_part.reshape(dp_count, CAP, features).astype(jnp.bfloat16),
        "dp",
        split_axis=0,
        concat_axis=0,
        tiled=True,
    ).astype(jnp.float32)
    y_slots = collect(y_back)
    dx_slots = collect(dx_back)
    mixed = jnp.dot(weighted.T, y_slots, precision=lax.Precision.HIGHEST).astype(jnp.bfloat16)
    grad_tokens = jnp.dot(pick_table.T, dx_slots, precision=lax.Precision.HIGHEST).astype(
        jnp.bfloat16
    )
    grad_up = g_up.astype(jnp.bfloat16).reshape(1, features, hidden_own)
    grad_down = g_down.astype(jnp.bfloat16).reshape(1, features, hidden_own)
    return (mixed, grad_tokens, grad_up, grad_down)


def slot_rows(routes_ref):
    tok = routes_ref.shape[1]
    expert = lax.broadcasted_iota(jnp.int32, (E, tok), 0)
    hits = [(routes_ref[k : k + 1, :] == expert) for k in range(2)]
    either = jnp.where(hits[0] | hits[1], 1.0, 0.0).astype(BF)
    earlier = lax.broadcasted_iota(jnp.int32, (tok, tok), 0) < lax.broadcasted_iota(
        jnp.int32, (tok, tok), 1
    )
    before = jnp.dot(either, jnp.where(earlier, 1.0, 0.0).astype(BF), preferred_element_type=F32)
    return [jnp.where(hit, before, NOWHERE) for hit in hits]


def padded(rows):
    return -(-rows // SUBLANES) * SUBLANES


def slot_hits(rows, e, count=CAP, base=0):
    slot = lax.broadcasted_iota(jnp.int32, (count, rows[0].shape[1]), 0).astype(F32)
    return [jnp.where(slot == rows[k][e : e + 1, :] + base, 1.0, 0.0) for k in range(2)]


def route_kernel(routes_ref, weights_ref, tokens_ref, cot_ref, out_ref, wide_ref):
    features = tokens_ref.shape[1]
    size = out_ref.shape[0] // HALVES
    half = features // HALVES
    rows = slot_rows(routes_ref)
    for e in range(E):
        at = slot_hits(rows, e)
        pick = (at[0] + at[1]).astype(BF)
        scale = jnp.sum(at[0] * weights_ref[0:1, :] + at[1] * weights_ref[1:2, :], 1, keepdims=True)
        x_rows = jnp.dot(pick, tokens_ref[...], preferred_element_type=F32)
        d_rows = scale * jnp.dot(pick, cot_ref[...], preferred_element_type=F32)
        other = e ^ size
        cut = (other // size) * half
        for i, value in enumerate((x_rows, d_rows)):
            wide_ref[e, i * CAP : (i + 1) * CAP, :] = value
            wide_ref[other, 2 * CAP : 3 * CAP, i * half : (i + 1) * half] = value[:, cut : cut + half]
    extra = out_ref.shape[1] - 3 * CAP
    for e in range(E):
        if extra:
            wide_ref[e, 3 * CAP :, :] = jnp.zeros((extra, features), F32)
        out_ref[e] = wide_ref[e].astype(BF)


def route(routes_t, weights_t, tokens, cotangent, dp_count):
    features = tokens.shape[1]
    return pl.pallas_call(
        route_kernel,
        out_shape=jax.ShapeDtypeStruct((dp_count, padded(3 * CAP), features), BF),
        scratch_shapes=[pltpu.VMEM((dp_count, padded(3 * CAP), features), F32)],
        cost_estimate=pl.CostEstimate(
            flops=4 * E * CAP * tokens.size, bytes_accessed=2 * 10 * tokens.size, transcendentals=0
        ),
        compiler_params=pltpu.CompilerParams(vmem_limit_bytes=KERNEL_VMEM),
        name="route",
    )(routes_t, weights_t, tokens, cotangent)


def returned(size, e, half, kind):
    near = e // size == half
    return (e if near else e ^ size), (kind if near else 2 + kind) * CAP


def mix_kernel(routes_ref, weights_ref, back_ref, mixed_ref, grad_ref):
    tok = routes_ref.shape[1]
    rows = slot_rows(routes_ref)
    owners, count, width = back_ref.shape
    for half in range(HALVES):
        first, second, grad = [jnp.zeros((tok, width), F32) for _ in range(3)]
        for e in range(E):
            owner, base = returned(owners // HALVES, e, half, 0)
            at = slot_hits(rows, e, count, base)
            first += contract(at[0].astype(BF), back_ref[owner], 0, 0)
            second += contract(at[1].astype(BF), back_ref[owner], 0, 0)
            owner, base = returned(owners // HALVES, e, half, 1)
            at = slot_hits(rows, e, count, base)
            grad += contract((at[0] + at[1]).astype(BF), back_ref[owner], 0, 0)
        lanes = slice(half * width, (half + 1) * width)
        mixed_ref[:, lanes] = (weights_ref[:, 0:1] * first + weights_ref[:, 1:2] * second).astype(BF)
        grad_ref[:, lanes] = grad.astype(BF)


def full_spec(shape):
    return pl.BlockSpec(shape, lambda q, where: (0,) * len(shape))


class Plan:
    def __init__(self, dp_count, members, share, hidden):
        self.dp_count, self.members, self.share, self.hidden = dp_count, members, share, hidden
        self.size = dp_count // HALVES
        self.peers = self.size - 1
        self.group_features = self.size * share
        self.slots = dp_count * CAP
        self.where = jnp.stack([lax.axis_index("dp"), lax.axis_index("member")]).astype(jnp.int32)
        self.last = None

    def part(self, where, p, k=0):
        return (where[0] ^ (p * self.size)) ^ k

    def swap(self, value, k):
        return lax.ppermute(value, "dp", [(i, i ^ k) for i in range(self.dp_count)])

    def pass_on(self, value, k):
        return lax.ppermute(value, "member", [(i, i ^ k) for i in range(self.members)])

    def call(self, kernel, grid, in_specs, args, out_specs, out_shape, cost, aliases=None, scratch=()):
        args, in_specs = list(args), list(in_specs)
        if self.last is not None and not any(arg is self.last for arg in args):
            args.append(self.last)
            in_specs.append(pl.BlockSpec(memory_space=pl.ANY))

            def placed(where, *refs, count=len(args) - 1):
                kernel(where, *refs[:count], *refs[count + 1 :])
        else:
            placed = kernel
        outs = pl.pallas_call(
            placed,
            grid_spec=pltpu.PrefetchScalarGridSpec(
                num_scalar_prefetch=1,
                grid=grid,
                in_specs=in_specs,
                out_specs=out_specs,
                scratch_shapes=scratch,
            ),
            out_shape=out_shape,
            input_output_aliases={i + 1: o for i, o in (aliases or {}).items()},
            cost_estimate=pl.CostEstimate(flops=cost[0], bytes_accessed=cost[1], transcendentals=0),
            compiler_params=pltpu.CompilerParams(vmem_limit_bytes=KERNEL_VMEM),
        )(self.where, *args)
        self.last = outs[-1]
        return outs


def prepare(plan, got):
    features = got.shape[2]
    half, share, slots = plan.group_features, plan.share, plan.slots

    def kernel(where, got_ref, own_ref, rows_ref, wide_ref):
        place, group = where[0] % plan.size, where[0] // plan.size
        for b in range(plan.dp_count):
            value = got_ref[b].astype(F32)
            for i in range(3):
                wide_ref[b * CAP : (b + 1) * CAP, i * features : (i + 1) * features] = value[
                    i * CAP : (i + 1) * CAP
                ]
        for i in range(2):
            own_ref[i] = wide_ref[:, i * features : (i + 1) * features].astype(BF)
            for k in range(plan.size):
                into = slice(k * share, (k + 1) * share)
                shift = (place ^ k) * share
                for p, base in ((0, i * features + group * half), (1, 2 * features + i * half)):
                    at = pl.multiple_of(base + shift, LANES)
                    rows_ref[2 * p + i, :, into] = wide_ref[:, pl.ds(at, share)].astype(BF)

    return plan.call(
        kernel,
        (1,),
        [full_spec(got.shape)],
        [got],
        [full_spec((2, slots, features)), full_spec((4, slots, half))],
        [
            jax.ShapeDtypeStruct((2, slots, features), BF),
            jax.ShapeDtypeStruct((4, slots, half), BF),
        ],
        (0, 4 * got.size),
        scratch=[pltpu.VMEM((slots, 3 * features), F32)],
    )


def pack(plan, up, down, start, width):
    step = plan.members * LANES
    first = start // step

    def kernel(where, *refs):
        del where
        sources, outs = refs[: plan.peers * 4], refs[-plan.peers :]
        for k in range(plan.peers):
            for i in range(4):
                outs[k][i] = sources[k * 4 + i][0]

    in_specs = [
        pl.BlockSpec(
            (1, plan.share, step),
            functools.partial(lambda i, where, p, k: (plan.part(where, p, k), 0, first + i), p=p, k=k),
        )
        for k in range(1, plan.size)
        for p in range(HALVES)
        for _ in range(2)
    ]
    return plan.call(
        kernel,
        (width // step,),
        in_specs,
        [up, down] * (plan.peers * HALVES),
        [
            pl.BlockSpec((4, plan.share, step), lambda i, where: (0, 0, i))
            for _ in range(plan.peers)
        ],
        [jax.ShapeDtypeStruct((4, plan.share, width), BF) for _ in range(plan.peers)],
        (0, plan.peers * 4 * plan.share * width * 4),
    )


def weight_specs(plan, start, width):
    own = pl.BlockSpec(
        (1, plan.share, width), lambda p, where: (plan.part(where, p), 0, start // width)
    )
    return [own, own] + [
        pl.BlockSpec((2, plan.share, width), lambda p, where: (p, 0, 0)) for _ in range(plan.peers)
    ]


def member_lanes(where, m, sub):
    return pl.ds(pl.multiple_of((where[1] ^ m) * sub, LANES), sub)


def member_groups(plan, sub):
    take = max(1, min(plan.members, 2 * LANES // sub))
    return [range(m, m + take) for m in range(0, plan.members, take)]


def stacked_rows(refs, i, lanes):
    return jnp.concatenate([refs[i][0, :, lanes]] + [ref[i, :, lanes] for ref in refs[2:]], axis=0)


def hidden_partials(plan, rows, up, down, came, start, width):
    sub = width // plan.members
    half, slots = plan.group_features, plan.slots

    def kernel(where, rows_ref, *refs):
        w_refs, outs = refs[: 2 + plan.peers], refs[-plan.members :]
        for ms in member_groups(plan, sub):
            for i in range(2):
                weights = [stacked_rows(w_refs, i, member_lanes(where, m, sub)) for m in ms]
                value = jnp.dot(
                    rows_ref[i], jnp.concatenate(weights, axis=1), preferred_element_type=F32
                ).astype(BF)
                for j, m in enumerate(ms):
                    outs[m][i] = value[:, j * sub : (j + 1) * sub]

    return plan.call(
        kernel,
        (HALVES,),
        [pl.BlockSpec((2, slots, half), lambda p, where: (p, 0, 0))]
        + weight_specs(plan, start, width),
        [rows, up, down, *came],
        [pl.BlockSpec((2, slots, sub), lambda p, where: (p, 0, 0)) for _ in range(plan.members)],
        [jax.ShapeDtypeStruct((4, slots, sub), BF) for _ in range(plan.members)],
        (8 * slots * half * width, 8 * width * (slots + half)),
    )


def sum_members(plan, parts):
    _, slots, sub = parts[0].shape

    def kernel(where, *refs):
        del where
        total = refs[0][...].astype(F32)
        for ref in refs[1 : plan.members]:
            total += ref[...].astype(F32)
        refs[-1][...] = total.astype(BF)

    spec = pl.BlockSpec((2, slots, sub), lambda p, where: (p, 0, 0))
    return plan.call(
        kernel,
        (HALVES,),
        [spec] * plan.members,
        parts,
        [spec],
        [jax.ShapeDtypeStruct((4, slots, sub), BF)],
        (0, 8 * slots * sub * (plan.members + 1)),
    )[0]


def activate(plan, sums, back):
    _, slots, sub = sums.shape

    def kernel(where, sums_ref, back_ref, *refs):
        del where
        pre, d_act = [sums_ref[i].astype(F32) + back_ref[i].astype(F32) for i in range(2)]
        sigma = 1.0 / (1.0 + jnp.exp(-pre))
        refs[-1][0] = (pre * sigma).astype(BF)
        refs[-1][1] = (d_act * sigma * (1.0 + pre * (1.0 - sigma))).astype(BF)

    spec = pl.BlockSpec((2, slots, sub), lambda p, where: (p, 0, 0))
    return plan.call(
        kernel,
        (HALVES,),
        [spec, pl.BlockSpec((2, slots, sub), lambda p, where: (1 - p, 0, 0))],
        [sums, back],
        [spec],
        [jax.ShapeDtypeStruct((4, slots, sub), BF)],
        (0, 24 * slots * sub),
    )[0]


def feature_sums(plan, total, pieces, up, down, came, start, width, final):
    sub = width // plan.members
    half, share, slots = plan.group_features, plan.share, plan.slots
    count = padded(4 * CAP)

    def kernel(where, *refs):
        place = where[0] % plan.size
        p_refs = refs[: plan.members]
        w_refs = refs[plan.members : plan.members + 2 + plan.peers]
        before = refs[plan.members + 2 + plan.peers]
        out, acc, wide = refs[-3:] if final else (refs[-1], None, None)
        for i in range(2):
            value = None
            for ms in member_groups(plan, sub):
                weights = [stacked_rows(w_refs, 1 - i, member_lanes(where, m, sub)) for m in ms]
                hidden = jnp.concatenate([p_refs[m][i] for m in ms], axis=1)
                term = contract(hidden, jnp.concatenate(weights, axis=1), 1, 1)
                value = term if value is None else value + term
            for k in range(plan.size):
                at = pl.ds(pl.multiple_of((place ^ k) * share, LANES), share)
                piece = value[:, k * share : (k + 1) * share]
                if total is not None:
                    piece += before[i, :, at]
                if final:
                    acc[:, at] = piece
                else:
                    out[i, :, at] = piece
            if final:
                for p in range(HALVES):

                    @pl.when(pl.program_id(0) == p)
                    def _(first=(2 * p + i) * CAP):
                        for b in range(plan.dp_count):
                            wide[b, first : first + CAP, :] = acc[b * CAP : (b + 1) * CAP, :]

        if final:

            @pl.when(pl.program_id(0) == HALVES - 1)
            def _():
                for b in range(plan.dp_count):
                    if count > 4 * CAP:
                        wide[b, 4 * CAP :, :] = jnp.zeros((count - 4 * CAP, half), F32)
                    out[b] = wide[b].astype(BF)

    stack = pl.BlockSpec((2, slots, half), lambda p, where: (p, 0, 0))
    in_specs = [
        pl.BlockSpec((2, slots, sub), lambda p, where: (p, 0, 0)) for _ in range(plan.members)
    ] + weight_specs(plan, start, width)
    args = [*pieces, up, down, *came]
    if total is not None:
        in_specs.append(stack)
        args.append(total)
    if final:
        shape = (plan.dp_count, count, half)
        out_spec, out = full_spec(shape), jax.ShapeDtypeStruct(shape, BF)
        scratch = [pltpu.VMEM((slots, half), F32), pltpu.VMEM(shape, F32)]
    else:
        out_spec, out, scratch = stack, jax.ShapeDtypeStruct((4, slots, half), F32), ()
    return plan.call(
        kernel,
        (HALVES,),
        in_specs,
        args,
        [out_spec],
        [out],
        (8 * slots * half * width, 8 * width * (slots + half) + 32 * slots * half),
        scratch=scratch,
    )[0]


def weight_grads(plan, buffers, x_t, d_t, pieces, start, width):
    sub = width // plan.members
    features, slots = x_t.shape
    block = features // GRAD_STEPS

    def kernel(where, x_ref, d_ref, *refs):
        up_out, down_out = refs[-2:]
        for ms in member_groups(plan, sub):
            for i, (rows_ref, out) in enumerate(((d_ref, down_out), (x_ref, up_out))):
                hidden = jnp.concatenate([refs[m][i] for m in ms], axis=1)
                value = jnp.dot(rows_ref[...], hidden, preferred_element_type=F32).astype(BF)
                for j, m in enumerate(ms):
                    out[0, :, member_lanes(where, m, sub)] = value[:, j * sub : (j + 1) * sub]

    in_specs = [pl.BlockSpec((block, slots), lambda q, where: (q, 0))] * 2
    in_specs += [full_spec((2, slots, sub))] * plan.members
    args = [x_t, d_t, *pieces]
    aliases = {}
    if buffers is not None:
        aliases = {len(args): 0, len(args) + 1: 1}
        in_specs += [pl.BlockSpec(memory_space=pl.ANY)] * 2
        args += buffers
    return plan.call(
        kernel,
        (GRAD_STEPS,),
        in_specs,
        args,
        [pl.BlockSpec((1, block, width), lambda q, where: (0, q, start // width))] * 2,
        [jax.ShapeDtypeStruct((1, features, plan.hidden), BF) for _ in range(2)],
        (4 * features * slots * width, 4 * width * (slots + features)),
        aliases=aliases,
    )


def chunk_list(hidden, unit):
    units = hidden // unit
    wide = max(0, (units - 6) // 2)
    narrow = [(2 * wide + i, 1) for i in range(units - 2 * wide)]
    chunks = narrow[:1] + [(2 * i, 2) for i in range(wide)] + narrow[1:]
    return [(unit * start, unit * width) for start, width in chunks]


LAGS = (
    ("hidden", 0),
    ("sums", 1),
    ("grads", 4),
    ("fetch", -2),
    ("activate", 2),
    ("features", 3),
)


def order_of(count):
    steps = [("fetch", 0), ("route", 0), ("fetch", 1), ("prepare", 0)]
    for i in range(count + max(lag for _, lag in LAGS)):
        for kind, lag in LAGS:
            first = 2 if kind == "fetch" else 0
            if first <= i - lag < count and (kind != "grads" or i < count):
                steps.append((kind, i - lag))
    steps.append(("return", 0))
    return steps + [("grads", i) for i in range(count) if ("grads", i) not in steps]


def halves_body(tokens, routes, route_weights, up, down, cotangent):
    dp_count, members = lax.axis_size("dp"), lax.axis_size("member")
    share, hidden = up.shape[1:]
    plan = Plan(dp_count, members, share, hidden)

    chunks = chunk_list(hidden, members * LANES)
    count = len(chunks)
    routes_t, weights_t = routes.T, route_weights.T

    came, reduced, summed, backs, pieces = {}, {}, {}, {}, {}
    got = own = rows = total = grads = back = None
    for kind, i in order_of(count):
        if kind == "fetch":
            packed = pack(plan, up, down, *chunks[i])
        elif kind == "route":
            send = route(routes_t, weights_t, tokens, cotangent, dp_count)
        elif kind == "prepare":
            own, rows = prepare(plan, got)
        elif kind == "hidden":
            outs = hidden_partials(plan, rows, up, down, came[i], *chunks[i])
        elif kind == "sums":
            summed[i] = sum_members(plan, reduced[i])
        elif kind == "activate":
            acts = activate(plan, summed[i], backs[i])
        elif kind == "features":
            total = feature_sums(
                plan, total, pieces[i], up, down, came[i], *chunks[i], i == count - 1
            )
        elif kind == "grads":
            grads = weight_grads(plan, grads, x_t, d_t, pieces[i], *chunks[i])
        if kind == "fetch":
            came[i] = [plan.swap(packed[k], k + 1) for k in range(plan.peers)]
        elif kind == "route":
            got = lax.all_to_all(send, "dp", split_axis=0, concat_axis=0, tiled=True)
        elif kind == "prepare":
            x_t, d_t = own[0].T, own[1].T
        elif kind == "hidden":
            reduced[i] = [outs[0]] + [plan.pass_on(outs[k], k) for k in range(1, members)]
        elif kind == "sums":
            backs[i] = plan.swap(summed[i], plan.size)
        elif kind == "activate":
            pieces[i] = [acts] + [plan.pass_on(acts, k) for k in range(1, members)]
        elif kind == "return":
            back = lax.all_to_all(total, "dp", split_axis=0, concat_axis=0, tiled=True)

    out = jax.ShapeDtypeStruct(tokens.shape, BF)
    mixed, grad_tokens = pl.pallas_call(
        mix_kernel,
        out_shape=(out, out),
        compiler_params=pltpu.CompilerParams(vmem_limit_bytes=KERNEL_VMEM),
        name="mix",
    )(routes_t, route_weights, back)
    return (mixed, grad_tokens, *grads)


def power_of_two(value):
    return value & (value - 1) == 0


def solution(mesh):
    placed = (
        P("dp", "member"),
        P("dp", None),
        P("dp", None),
        P(None, ("member", "dp"), None),
        P(None, ("member", "dp"), None),
        P("dp", "member"),
    )

    dp_count, members = mesh.shape["dp"], mesh.shape["member"]
    fits = (
        dp_count == E
        and power_of_two(members)
        and FF_W % (members * LANES) == 0
    )

    def body(*args):
        if not fits or args[3].shape[1] % LANES:
            return plain_body(*args)
        return halves_body(*args)

    return jax.shard_map(
        body,
        mesh=mesh,
        in_specs=placed,
        out_specs=(
            P("dp", "member"),
            P("dp", "member"),
            P("dp", "member", None),
            P("dp", "member", None),
        ),
        check_vma=False,
    )
```
